1024 devices in a mesh: dp: 64 (over y, x), ctx: 16 (over z, core).
Axes of the slice: x: 8, y: 8, z: 8, core: 2. Of those that a mesh axis runs over, the one named last changes fastest.
Arguments:
- queries: bfloat16 [131072, 512], P(('dp', 'ctx')), may hold values from -25 to 25
- keys: bfloat16 [131072, 128], P(('dp', 'ctx')), may hold values from -6 to 6
- values: bfloat16 [131072, 128], P(('dp', 'ctx')), may hold values from -6 to 6
- out_grad: bfloat16 [131072, 512], P(('dp', 'ctx')), may hold values from -7 to 7
- doc_lengths: int32 [64, 65], P('dp'), may hold values from 0 to 2048, as said below
- source_slot: int32 [131072], P(('dp', 'ctx')), may hold values from 0 to 127, as said below
Outputs:
- attended: bfloat16 [131072, 512], P(('dp', 'ctx'))
- query_grad: bfloat16 [131072, 512], P(('dp', 'ctx'))
- key_grad: bfloat16 [131072, 128], P(('dp', 'ctx'))
- value_grad: bfloat16 [131072, 128], P(('dp', 'ctx'))
The draws below stay inside these ranges and needn't reach their ends.
Inputs may be any that keep to these rules, and one draw needn't show every extreme that they name: `doc_lengths`: row d lists group d's documents in order: the first covers devices 0 to m - 1 of the group whole (m * 128 tokens, 1 <= m <= 16, with m = 16 in row 0), then 4 documents of positive length for each later device that fill that device exactly, then zeros; every row sums to 2048. `source_slot`: on each device the 128 entries are a permutation of 0 to 127.
All inputs are finite; a program needn't handle non-finite values.
Results may differ from the reference program's by a relative error of at most 0.033.
Values may be sent and summed in bfloat16 or wider, within the bound.
A program may use at most 32 MiB of HBM per device.

```python
import jax
import jax.numpy as jnp
from jax import lax

DH = 128
HQ = 4
TOK_DEV = 128
SHORT_DEV = 4
GROUP = 2048
TOKENS = 131072
N_DP = 64
N_CTX = 16


def plan_slots(key):
    devices = TOKENS // TOK_DEV
    raw_scores = jax.random.randint(jax.random.fold_in(key, 11), (devices, TOK_DEV), 0, 2 ** 20, dtype=jnp.int32)
    raw_scores = raw_scores * TOK_DEV + jnp.arange(TOK_DEV, dtype=jnp.int32)[None, :]
    return jnp.argsort(raw_scores, axis=1).astype(jnp.int32).reshape(TOKENS)


def arrival_index_drawn(slots):
    ctx_count = GROUP // TOK_DEV
    peer_rows = TOK_DEV // (TOKENS // GROUP)
    global_row = jnp.arange(TOKENS, dtype=jnp.int32)
    device = global_row // TOK_DEV
    group_index = device // ctx_count
    ctx_index = device % ctx_count
    return (slots // peer_rows * ctx_count + ctx_index) * TOK_DEV + group_index * peer_rows + slots % peer_rows


def doc_table(key):
    group_count = TOKENS // GROUP
    ctx_count = GROUP // TOK_DEV
    span_devices = jax.random.randint(jax.random.fold_in(key, 21), (group_count,), 1, ctx_count + 1, dtype=jnp.int32)
    span_devices = span_devices.at[0].set(ctx_count)
    candidates = TOK_DEV - 1
    raw_scores = jax.random.randint(jax.random.fold_in(key, 22), (group_count, ctx_count, candidates), 0, 2 ** 20, dtype=jnp.int32)
    raw_scores = raw_scores * candidates + jnp.arange(candidates, dtype=jnp.int32)[None, None, :]
    cut_points = jnp.sort(jnp.argsort(raw_scores, axis=2)[:, :, :SHORT_DEV - 1].astype(jnp.int32) + 1, axis=2)
    bounds = jnp.concatenate([jnp.zeros((group_count, ctx_count, 1), jnp.int32), cut_points, jnp.full((group_count, ctx_count, 1), TOK_DEV, jnp.int32)], axis=2)
    short_lengths = (bounds[:, :, 1:] - bounds[:, :, :-1]).reshape(group_count, ctx_count * SHORT_DEV)
    shifted = jnp.arange(ctx_count * SHORT_DEV, dtype=jnp.int32)[None, :] + span_devices[:, None] * SHORT_DEV
    taken_lengths = jnp.take_along_axis(short_lengths, jnp.minimum(shifted, ctx_count * SHORT_DEV - 1), axis=1)
    taken_lengths = jnp.where(shifted < ctx_count * SHORT_DEV, taken_lengths, 0)
    return jnp.concatenate([span_devices[:, None] * TOK_DEV, taken_lengths], axis=1).astype(jnp.int32)


def drawn_rows(key):
    key_rows = jax.random.truncated_normal(jax.random.fold_in(key, 31), -6.0, 6.0, (TOKENS, DH), jnp.float32)
    query_rows = jax.random.truncated_normal(jax.random.fold_in(key, 32), -6.0, 6.0, (TOKENS, HQ * DH), jnp.float32)
    return (query_rows, key_rows)


def draw_queries(key, part):
    query_rows, key_rows = drawn_rows(key)
    target = arrival_index_drawn(plan_slots(key))
    return jnp.zeros((TOKENS, HQ * DH), jnp.float32).at[target].set(query_rows).astype(jnp.bfloat16)


def draw_keys(key, part):
    query_rows, key_rows = drawn_rows(key)
    target = arrival_index_drawn(plan_slots(key))
    return jnp.zeros((TOKENS, DH), jnp.float32).at[target].set(key_rows).astype(jnp.bfloat16)


def draw_out_grad(key, part):
    ctx_count = GROUP // TOK_DEV
    noise = jax.random.truncated_normal(jax.random.fold_in(key, 41), -6.0, 6.0, (TOKENS, HQ * DH), jnp.float32)
    column_signs = (2 * jax.random.randint(jax.random.fold_in(key, 42), (HQ * DH,), 0, 2, dtype=jnp.int32) - 1).astype(jnp.float32)
    global_row = jnp.arange(TOKENS, dtype=jnp.int32)
    ctx_index = global_row // TOK_DEV % ctx_count
    later = (2 * ctx_index >= ctx_count).astype(jnp.float32)
    grad_rows = noise + later[:, None] * column_signs[None, :]
    target = arrival_index_drawn(plan_slots(key))
    return jnp.zeros((TOKENS, HQ * DH), jnp.float32).at[target].set(grad_rows).astype(jnp.bfloat16)


def draw_doc_lengths(key, part):
    return doc_table(key)


def draw_source_slot(key, part):
    return plan_slots(key)


def levels(rng, shape, cuts, smallest, top_value):
    def one(axis_at, shards_of):
        steps = jax.random.uniform(jax.random.fold_in(jax.random.fold_in(rng, 6), axis_at), (shards_of,), jnp.float32, smallest / len(cuts), top_value / len(cuts))
        return jnp.repeat(jnp.exp(steps), shape[axis_at] // shards_of).reshape((-1,) + (1,) * (len(shape) - axis_at - 1))

    gain = one(*cuts[0])
    for cut in cuts[1:]:
        gain = gain * one(*cut)
    return gain


def normal_values(key, dims, scale, limit, pieces=(), held_as=jnp.bfloat16):
    entries = scale * jax.random.normal(key, dims, jnp.float32)
    if pieces:
        entries = entries * levels(key, dims, pieces, -0.22, 0.18)
    return jnp.clip(entries, -limit, limit).astype(held_as)


def setup_inputs(seed: int = 0) -> dict:
    seeds = jax.random.split(jax.random.key(seed), 7)
    queries = draw_queries(jax.random.fold_in(seeds[6], 71), 0)
    keys = draw_keys(jax.random.fold_in(seeds[6], 71), 0)
    values = normal_values(seeds[2], (TOKENS, DH), 1.0, 6.0, ((0, 1024),))
    out_grad = draw_out_grad(jax.random.fold_in(seeds[6], 71), 0)
    doc_lengths = draw_doc_lengths(jax.random.fold_in(seeds[6], 71), 0)
    source_slot = draw_source_slot(jax.random.fold_in(seeds[6], 71), 0)
    return dict(queries=queries, keys=keys, values=values, out_grad=out_grad, doc_lengths=doc_lengths, source_slot=source_slot)


def arrival_index(source_slot):
    peer_rows = TOK_DEV // N_DP
    global_row = jnp.arange(TOKENS, dtype=jnp.int32)
    device = global_row // TOK_DEV
    group_index = device // N_CTX
    ctx_index = device % N_CTX
    return ((source_slot // peer_rows) * N_CTX + ctx_index) * TOK_DEV + group_index * peer_rows + source_slot % peer_rows


def narrowed(values_in):
    rounded = values_in.astype(jnp.bfloat16)
    return lax.optimization_barrier(rounded).astype(jnp.float32)


def one_group(group_data):
    query_rows, key_rows, value_rows, grad_rows, lengths = group_data
    score_scale = DH ** -0.5
    position = jnp.arange(GROUP, dtype=jnp.int32)
    doc_ends = jnp.cumsum(lengths, dtype=jnp.int32)
    doc = jnp.sum((position[:, None] >= doc_ends[None, :]).astype(jnp.int32), axis=1, dtype=jnp.int32)
    seen = (doc[:, None] == doc[None, :]) & (position[None, :] <= position[:, None])
    query_f = query_rows.astype(jnp.float32)
    key_f = key_rows.astype(jnp.float32)
    value_f = value_rows.astype(jnp.float32)
    grad_f = grad_rows.astype(jnp.float32)
    scores = jnp.einsum("thd,sd->hts", query_f, key_f) * score_scale
    log_total = jax.nn.logsumexp(jnp.where(seen[None], scores, -jnp.inf), axis=2)
    probs = jnp.where(seen[None], jnp.exp(scores - log_total[:, :, None]), 0.0)
    probs_low = narrowed(probs)
    attended = jnp.einsum("hts,sd->thd", probs_low, value_f).astype(jnp.bfloat16)
    row_delta = jnp.sum(grad_f * attended.astype(jnp.float32), axis=2)
    prob_grad = jnp.einsum("thd,sd->hts", grad_f, value_f)
    score_grad = narrowed(probs * (prob_grad - row_delta.T[:, :, None]))
    query_grad = (jnp.einsum("hts,sd->thd", score_grad, key_f) * score_scale).astype(jnp.bfloat16)
    key_grad = (jnp.einsum("hts,thd->sd", score_grad, query_f) * score_scale).astype(jnp.bfloat16)
    value_grad = jnp.einsum("hts,thd->sd", probs_low, grad_f).astype(jnp.bfloat16)
    return attended, query_grad, key_grad, value_grad


def reference(queries, keys, values, out_grad, doc_lengths, source_slot):
    target = arrival_index(source_slot)
    query_rows = queries[target].reshape(N_DP, GROUP, HQ, DH)
    key_rows = keys[target].reshape(N_DP, GROUP, DH)
    value_rows = values[target].reshape(N_DP, GROUP, DH)
    grad_rows = out_grad[target].reshape(N_DP, GROUP, HQ, DH)
    attended, query_grad, key_grad, value_grad = lax.map(one_group, (query_rows, key_rows, value_rows, grad_rows, doc_lengths))

    def placed(computed, template):
        return jnp.zeros_like(template).at[target].set(computed.reshape(template.shape))

    return (placed(attended, queries), placed(query_grad, queries), placed(key_grad, keys), placed(value_grad, values))
```

```python
import functools
import math

import jax
import jax.numpy as jnp
from jax import lax
from jax.experimental import pallas as pl
from jax.experimental.pallas import tpu as pltpu
from jax.sharding import PartitionSpec as P

MESH = pl.DeviceIdType.MESH
NEG = -1e30
F32 = jnp.float32
BF16 = jnp.bfloat16


def mm(left, right):
    return jnp.dot(left, right, preferred_element_type=F32)


def mm_nt(left, right):
    return lax.dot_general(left, right, (((1,), (1,)), ((), ())), preferred_element_type=F32)


def iota(shape, dim):
    return lax.broadcasted_iota(jnp.int32, shape, dim)


def far_first(n):
    order = sorted(range(1, n), key=lambda k: -min(k, n - k))
    return order


def kernel(
    ny, nx, nz, heads,
    q_hbm, k_hbm, v_hbm, g_hbm, lens_ref, slot_ref,
    o_out, dq_out, dk_out, dv_out,
    in_kv, in_qg, y_kv, y_qg, x_kv, x_qg, kv_all, qg,
    qf, gf, gt, s_all, dp_all, bias, lens_pad, m_row, l_row, o_t, dq_t,
    x_out, r_out, z_out, f_out, part, sib_part, comb, acc, z_kv, f_kv,
    in_sem, y_send, y_recv, xz_send, xz_recv, qg_send, qg_recv, fwd_send, fwd_recv,
    xo_send, xo_recv, yo_send, yo_recv, yk_send, yk_recv, part_send, part_recv, acc_send, acc_recv,
    ready,
):
    tok = in_kv.shape[0]
    dh = k_hbm.shape[1]
    wide = heads * dh
    peer = tok // (ny * nx)
    blk = tok // ny
    scale = dh ** -0.5
    dp = lax.axis_index("dp")
    ctx = lax.axis_index("ctx")
    y, x = dp // nx, dp % nx
    z, core = ctx // 2, ctx % 2
    sibling = (dp, z * 2 + 1 - core)

    def at(yy, xx, zz):
        return (yy * nx + xx, zz * 2 + core)

    def rows(i):
        return pl.ds(pl.multiple_of(i * blk, blk), blk)

    def remote(src, dst, send, recv, dev):
        return pltpu.make_async_remote_copy(
            src_ref=src, dst_ref=dst, send_sem=send, recv_sem=recv, device_id=dev, device_id_type=MESH
        )

    def drain(ref, sem):
        pltpu.make_async_copy(ref, ref, sem).wait()

    loads = [
        pltpu.make_async_copy(k_hbm, in_kv.at[:, pl.ds(0, dh)], in_sem.at[0]),
        pltpu.make_async_copy(v_hbm, in_kv.at[:, pl.ds(dh, dh)], in_sem.at[1]),
        pltpu.make_async_copy(q_hbm, in_qg.at[:, pl.ds(0, wide)], in_sem.at[2]),
        pltpu.make_async_copy(g_hbm, in_qg.at[:, pl.ds(wide, wide)], in_sem.at[3]),
    ]
    for load in loads:
        load.start()

    barrier = pltpu.get_barrier_semaphore()
    for k in far_first(ny):
        pl.semaphore_signal(barrier, inc=1, device_id=at((y + k) % ny, x, z), device_id_type=MESH)
    for k in far_first(nx):
        pl.semaphore_signal(barrier, inc=1, device_id=at(y, (x + k) % nx, z), device_id_type=MESH)
    for k in far_first(nz):
        pl.semaphore_signal(barrier, inc=1, device_id=at(y, x, (z + k) % nz), device_id_type=MESH)
    pl.semaphore_signal(barrier, inc=1, device_id=sibling, device_id_type=MESH)
    for load in loads:
        load.wait()
    pl.semaphore_wait(barrier, ny + nx + nz - 2)

    for i, (src, dst) in enumerate(((in_kv, y_kv), (in_qg, y_qg))):
        for k in far_first(ny):
            t = (y + k) % ny
            remote(src.at[rows(t)], dst.at[rows(y)], y_send.at[i], y_recv.at[i], at(t, x, z)).start()
        dst[rows(y), :] = src[rows(y), :]
    for k in far_first(nx):
        pl.semaphore_signal(ready, inc=1, device_id=at(y, (x + k) % nx, z), device_id_type=MESH)

    row_i, col_i = iota((tok, tok), 0), iota((tok, tok), 1)
    swapped = (row_i // peer % nx) * blk + (row_i // blk) * peer + row_i % peer
    regroup = (swapped == col_i).astype(BF16)
    eye = (row_i == col_i).astype(F32)
    eye_low = eye.astype(BF16)

    slot = slot_ref[...]
    arrived = (slot // peer % nx) * blk + (slot // blk) * peer + slot % peer
    pos_col = jnp.sum(jnp.where(row_i == arrived, col_i.astype(F32), 0.0), axis=1, keepdims=True)
    pos_row = jnp.sum(eye * pos_col, axis=0, keepdims=True)
    lens_pad[...] = jnp.zeros_like(lens_pad)
    lens_pad[:, pl.ds(0, lens_ref.shape[1])] = lens_ref[...].astype(F32)
    lens = lens_pad[...]
    pad = lens.shape[1]
    below = iota((pad, pad), 1) <= iota((pad, pad), 0)
    ends_col = jnp.sum(jnp.where(below, lens, 0.0), axis=1, keepdims=True)
    first = (ctx * tok).astype(F32)
    doc_row = jnp.sum((ends_col <= pos_row + first).astype(F32), axis=0, keepdims=True)
    doc_col = jnp.sum(eye * doc_row, axis=1, keepdims=True)
    seen = (doc_col == doc_row) & (pos_col <= pos_row)
    own = jnp.where(seen, 0.0, NEG)
    later = jnp.where(lens[:, :1] >= first + tok, 0.0, NEG) + jnp.zeros((tok, tok), F32)
    bias[0, pl.ds(0, tok), :] = jnp.where(core == 0, own, later)
    bias[0, pl.ds(tok, tok), :] = jnp.where(core == 0, NEG, own)
    bias[1, pl.ds(0, tok), :] = later
    bias[1, pl.ds(tok, tok), :] = later

    drain(y_kv.at[pl.ds(0, tok - blk)], y_recv.at[0])
    x_kv[...] = mm(regroup, y_kv[...]).astype(BF16)
    pl.semaphore_wait(ready, nx - 1)

    def offset(t):
        return jnp.where(t % 2 == 1, (t + 1) // 2, (nz - t // 2) % nz)

    def kv_out(i, carry):
        o = offset(nz - 1 - i)

        @pl.when(z + o < nz)
        def _():
            for k in range(nx):
                t = (x + k) % nx

                def send():
                    remote(
                        x_kv.at[rows(t)], kv_all.at[ctx, rows(x)], xz_send.at[z + o], xz_recv.at[z], at(y, t, z + o)
                    ).start()

                if k == 0:
                    pl.when(o > 0)(send)
                else:
                    send()

        return carry

    lax.fori_loop(0, nz, kv_out, 0)
    kv_all[ctx, rows(x), :] = x_kv[rows(x), :]

    drain(y_qg.at[pl.ds(0, tok - blk)], y_recv.at[1])
    x_qg[...] = mm(regroup, y_qg[...]).astype(BF16)
    for k in far_first(nx):
        t = (x + k) % nx
        remote(x_qg.at[rows(t)], qg.at[rows(x)], qg_send, qg_recv, at(y, t, z)).start()
    qg[rows(x), :] = x_qg[rows(x), :]

    def kv_forward(zz):
        here = zz * 2 + core

        @pl.when(zz == z)
        def _():
            drain(x_kv.at[pl.ds(0, tok - blk)], xz_recv.at[zz])

        @pl.when(zz != z)
        def _():
            drain(x_kv, xz_recv.at[zz])

        remote(kv_all.at[here], kv_all.at[here], fwd_send.at[zz], fwd_recv.at[zz], sibling).start()

    kv_forward(z)
    m_row[...] = jnp.full_like(m_row, NEG)
    l_row[...] = jnp.zeros_like(l_row)
    o_t[...] = jnp.zeros_like(o_t)
    dq_t[...] = jnp.zeros_like(dq_t)

    drain(qg.at[pl.ds(0, tok - blk)], qg_recv)
    for h in range(heads):
        cols = pl.ds(h * dh, dh)
        grad = qg[:, pl.ds(wide + h * dh, dh)]
        qf[pl.ds(h * tok, tok), :] = qg[:, cols]
        gf[pl.ds(h * tok, tok), :] = grad
        gt[:, pl.ds(h * tok, tok)] = mm_nt(eye_low, grad)

    def pair(zz):
        both = kv_all[pl.ds(zz * 2, 2)].reshape(2 * tok, 2 * dh)
        return both[:, :dh], both[:, dh:]

    def forward(t, carry):
        o = offset(t)
        nxt = offset(t + 1)

        @pl.when((t + 1 < nz) & (z >= nxt))
        def _():
            kv_forward(z - nxt)

        @pl.when(z >= o)
        def _():
            zz = z - o
            drain(x_kv, fwd_recv.at[zz])
            key, value = pair(zz)
            shift = bias[jnp.minimum(o, 1)]
            score = mm_nt(key, qf[...]) * scale + jnp.concatenate([shift] * heads, axis=1)
            s_all[zz] = score
            dp_all[zz] = mm_nt(value, gf[...])
            old = m_row[...]
            new = jnp.maximum(old, jnp.max(score, axis=0, keepdims=True))
            weight = jnp.exp(score - new)
            fade = jnp.exp(old - new)
            m_row[...] = new
            l_row[...] = l_row[...] * fade + jnp.sum(weight, axis=0, keepdims=True)
            value_t = mm_nt(eye_low, value).astype(BF16)
            o_t[...] = o_t[...] * fade + mm(value_t, weight.astype(BF16))

        return carry

    lax.fori_loop(0, nz, forward, 0)

    attended_t = (o_t[...] * (1.0 / l_row[...])).astype(BF16)
    delta = jnp.sum(gt[...] * attended_t.astype(F32), axis=0, keepdims=True)
    log_total = m_row[...] + jnp.log(l_row[...])

    def send_x(i, value_t):
        for h in range(heads):
            x_out[i, :, pl.ds(h * dh, dh)] = mm_nt(eye_low, value_t[:, h * tok : (h + 1) * tok]).astype(BF16)
        for k in far_first(nx):
            t = (x + k) % nx
            remote(x_out.at[i, rows(t)], r_out.at[i, rows(x)], xo_send.at[i], xo_recv.at[i], at(y, t, z)).start()
        r_out[i, rows(x), :] = x_out[i, rows(x), :]

    def send_y(i):
        drain(r_out.at[i, pl.ds(0, tok - blk)], xo_recv.at[i])
        z_out[i] = mm(regroup, r_out[i]).astype(BF16)
        for k in far_first(ny):
            t = (y + k) % ny
            remote(z_out.at[i, rows(t)], f_out.at[i, rows(y)], yo_send.at[i], yo_recv.at[i], at(t, x, z)).start()
        f_out[i, rows(y), :] = z_out[i, rows(y), :]

    send_x(0, attended_t)

    def share(zz):
        drain(x_kv, part_recv.at[zz])
        comb[zz] = (part[zz, core].astype(F32) + sib_part[zz].astype(F32)).astype(BF16)
        for k in range(nx):
            t = (x + k) % nx

            def send():
                remote(
                    comb.at[zz, rows(t)], acc.at[z, rows(x)], acc_send.at[zz], acc_recv.at[z], at(y, t, zz)
                ).start()

            if k == 0:
                pl.when(zz < z)(send)
            else:
                send()

    def backward(i, carry):
        t = nz - 1 - i
        o = offset(t)
        last = offset(t + 1)

        @pl.when(z >= o)
        def _():
            zz = z - o
            key, value = pair(zz)
            prob = jnp.exp(s_all[zz] - log_total)
            score_grad = (prob * (dp_all[zz] - delta)).astype(BF16)
            key_t = mm_nt(eye_low, key).astype(BF16)
            value_part = mm(prob.astype(BF16), gf[...])
            key_part = mm(score_grad, qf[...]) * scale
            dq_t[...] += mm(key_t, score_grad)
            for b in range(2):
                part[zz, b, :, pl.ds(0, dh)] = key_part[b * tok : (b + 1) * tok].astype(BF16)
                part[zz, b, :, pl.ds(dh, dh)] = value_part[b * tok : (b + 1) * tok].astype(BF16)
            remote(part.at[zz, 1 - core], sib_part.at[zz], part_send.at[zz], part_recv.at[zz], sibling).start()

        @pl.when((t + 1 < nz) & (z >= last))
        def _():
            share(z - last)

        return carry

    lax.fori_loop(0, nz, backward, 0)
    send_x(1, (dq_t[...] * scale).astype(BF16))
    share(z)
    acc[z, rows(x), :] = comb[z, rows(x), :]
    send_y(0)

    total = jnp.zeros((tok, 2 * dh), F32)
    y_kv_sum = y_kv
    for zz in range(nz):

        @pl.when(zz > z)
        def _():
            drain(x_kv, acc_recv.at[zz])

        @pl.when(zz == z)
        def _():
            drain(x_kv.at[pl.ds(0, tok - blk)], acc_recv.at[zz])

        @pl.when(zz < z)
        def _():
            acc[zz] = jnp.zeros((tok, 2 * dh), BF16)

        total = total + acc[zz].astype(F32)
    z_kv[...] = mm(regroup, total.astype(BF16)).astype(BF16)
    for k in far_first(ny):
        t = (y + k) % ny
        remote(z_kv.at[rows(t)], f_kv.at[rows(y)], yk_send, yk_recv, at(t, x, z)).start()
    f_kv[rows(y), :] = z_kv[rows(y), :]
    send_y(1)

    for i, ref in enumerate((in_kv, in_qg)):
        drain(ref.at[pl.ds(0, tok - blk)], y_send.at[i])
    drain(x_qg.at[pl.ds(0, tok - blk)], qg_send)
    for zz in range(nz):

        @pl.when(zz > z)
        def _():
            drain(x_kv, xz_send.at[zz])

        @pl.when(zz == z)
        def _():
            drain(x_kv.at[pl.ds(0, tok - blk)], xz_send.at[zz])
            drain(x_kv.at[pl.ds(0, tok - blk)], acc_send.at[zz])

        @pl.when(zz < z)
        def _():
            drain(x_kv, acc_send.at[zz])

        @pl.when(zz <= z)
        def _():
            drain(x_kv, fwd_send.at[zz])
            drain(x_kv, part_send.at[zz])

    for i in range(2):
        drain(x_out.at[i, pl.ds(0, tok - blk)], xo_send.at[i])
        drain(z_out.at[i, pl.ds(0, tok - blk)], yo_send.at[i])
    drain(z_kv.at[pl.ds(0, tok - blk)], yk_send)
    drain(f_out.at[0, pl.ds(0, tok - blk)], yo_recv.at[0])
    o_out[...] = f_out[0]
    drain(f_kv.at[pl.ds(0, tok - blk)], yk_recv)
    dk_out[...] = f_kv[:, :dh]
    dv_out[...] = f_kv[:, dh:]
    drain(f_out.at[1, pl.ds(0, tok - blk)], yo_recv.at[1])
    dq_out[...] = f_out[1]


def local(ny, nx, nz, queries, keys, values, out_grad, doc_lengths, source_slot):
    tok, dh = keys.shape
    wide = queries.shape[1]
    heads = wide // dh
    flat = heads * tok
    pad = -(-doc_lengths.shape[1] // 128) * 128
    dma = pltpu.SemaphoreType.DMA
    hbm = pl.BlockSpec(memory_space=pltpu.MemorySpace.HBM)
    vmem = pl.BlockSpec(memory_space=pltpu.VMEM)
    low = lambda *shape: pltpu.VMEM(shape, BF16)
    full = lambda *shape: pltpu.VMEM(shape, F32)
    return pl.pallas_call(
        functools.partial(kernel, ny, nx, nz, heads),
        out_shape=(
            jax.ShapeDtypeStruct((tok, wide), BF16),
            jax.ShapeDtypeStruct((tok, wide), BF16),
            jax.ShapeDtypeStruct((tok, dh), BF16),
            jax.ShapeDtypeStruct((tok, dh), BF16),
        ),
        in_specs=[hbm] * 4 + [vmem] * 2,
        out_specs=[vmem] * 4,
        scratch_shapes=[
            low(tok, 2 * dh), low(tok, 2 * wide),
            low(tok, 2 * dh), low(tok, 2 * wide),
            low(tok, 2 * dh), low(tok, 2 * wide),
            low(2 * nz, tok, 2 * dh), low(tok, 2 * wide),
            low(flat, dh), low(flat, dh), full(dh, flat),
            full(nz, 2 * tok, flat), full(nz, 2 * tok, flat),
            full(2, 2 * tok, tok), full(1, pad),
            full(1, flat), full(1, flat), full(dh, flat), full(dh, flat),
            low(2, tok, wide), low(2, tok, wide), low(2, tok, wide), low(2, tok, wide),
            low(nz, 2, tok, 2 * dh), low(nz, tok, 2 * dh), low(nz, tok, 2 * dh),
            low(nz, tok, 2 * dh), low(tok, 2 * dh), low(tok, 2 * dh),
            dma((4,)), dma((2,)), dma((2,)), dma((nz,)), dma((nz,)), dma(()), dma(()), dma((nz,)), dma((nz,)),
            dma((2,)), dma((2,)), dma((2,)), dma((2,)), dma(()), dma(()), dma((nz,)), dma((nz,)), dma((nz,)), dma((nz,)),
            pltpu.SemaphoreType.REGULAR,
        ],
        compiler_params=pltpu.CompilerParams(collective_id=0, has_side_effects=True),
        name="packed_attention",
    )(queries, keys, values, out_grad, doc_lengths, source_slot.reshape(1, tok))


def solution(mesh):
    side = math.isqrt(mesh.shape["dp"])
    placed = (
        P(("dp", "ctx"), None),
        P(("dp", "ctx"), None),
        P(("dp", "ctx"), None),
        P(("dp", "ctx"), None),
        P("dp", None),
        P(("dp", "ctx")),
    )
    return jax.shard_map(
        functools.partial(local, side, side, mesh.shape["ctx"] // 2),
        mesh=mesh,
        in_specs=placed,
        out_specs=(
            P(("dp", "ctx"), None),
            P(("dp", "ctx"), None),
            P(("dp", "ctx"), None),
            P(("dp", "ctx"), None),
        ),
        check_vma=False,
    )
```

```python
import functools
import math

import jax
import jax.numpy as jnp
from jax import lax
from jax.experimental import pallas as pl
from jax.experimental.pallas import tpu as pltpu
from jax.sharding import PartitionSpec as P

MESH = pl.DeviceIdType.MESH
NEG = -1e30
F32 = jnp.float32
BF16 = jnp.bfloat16


def OUT(*shape):
    return pltpu.VMEM(shape, BF16)


def mm(left, right):
    return jnp.dot(left, right, preferred_element_type=F32)


def mm_nt(left, right):
    return lax.dot_general(left, right, (((1,), (1,)), ((), ())), preferred_element_type=F32)


def iota(shape, dim):
    return lax.broadcasted_iota(jnp.int32, shape, dim)


def far_first(n):
    order = sorted(range(1, n), key=lambda k: -min(k, n - k))
    return order


def kernel(
    ny, nx, nz, heads,
    q_hbm, k_hbm, v_hbm, g_hbm, lens_hbm, slot_hbm,
    f_o, f_dq, f_kv,
    in_kv, in_q, in_g, lens_in, slot_in, y_kv, y_q, x_g, s_kv, s_q, s_g0, s_g, kv_all, q_all, g_all,
    qf, gf, gt, s_all, dp_all, bias, lens_pad, m_row, l_row, o_t, dq_t,
    x_out, r_out, z_out, part, sib_part, comb, acc, s_dkv, r_dkv, z_dkv,
    in_sem, a_send, a_recv, b_send, b_recv, z_send, z_recv, fwd_send, fwd_recv,
    xo_send, xo_recv, yo_send, yo_recv, part_send, part_recv, acc_send, acc_recv,
):
    tok = in_kv.shape[0]
    dh = k_hbm.shape[1]
    wide = heads * dh
    peer = tok // (ny * nx)
    blk = tok // ny
    scale = dh ** -0.5
    dp = lax.axis_index("dp")
    ctx = lax.axis_index("ctx")
    y, x = dp // nx, dp % nx
    z, core = ctx // 2, ctx % 2
    sibling = (dp, z * 2 + 1 - core)

    def at(yy, xx, zz):
        return (yy * nx + xx, zz * 2 + core)

    def rows(i):
        return pl.ds(pl.multiple_of(i * blk, blk), blk)

    def remote(src, dst, send, recv, dev):
        return pltpu.make_async_remote_copy(
            src_ref=src, dst_ref=dst, send_sem=send, recv_sem=recv, device_id=dev, device_id_type=MESH
        )

    def drain(ref, sem):
        pltpu.make_async_copy(ref, ref, sem).wait()

    def others(ref):
        return ref.at[pl.ds(0, tok - blk)]

    def along(axis, src, dst, send, recv):
        me = y if axis == "y" else x
        n = ny if axis == "y" else nx
        for k in far_first(n):
            t = (me + k) % n
            dev = at(t, x, z) if axis == "y" else at(y, t, z)
            remote(src.at[rows(t)], dst.at[rows(me)], send, recv, dev).start()
        dst[rows(me), :] = src[rows(me), :]

    barrier = pltpu.get_barrier_semaphore()
    for k in far_first(ny):
        pl.semaphore_signal(barrier, inc=1, device_id=at((y + k) % ny, x, z), device_id_type=MESH)
    for k in far_first(nx):
        pl.semaphore_signal(barrier, inc=1, device_id=at(y, (x + k) % nx, z), device_id_type=MESH)
    for k in far_first(nz):
        pl.semaphore_signal(barrier, inc=1, device_id=at(y, x, (z + k) % nz), device_id_type=MESH)
    pl.semaphore_signal(barrier, inc=1, device_id=sibling, device_id_type=MESH)

    loads = [
        pltpu.make_async_copy(g_hbm, in_g, in_sem.at[0]),
        pltpu.make_async_copy(k_hbm, in_kv.at[:, pl.ds(0, dh)], in_sem.at[1]),
        pltpu.make_async_copy(v_hbm, in_kv.at[:, pl.ds(dh, dh)], in_sem.at[2]),
        pltpu.make_async_copy(q_hbm, in_q, in_sem.at[3]),
        pltpu.make_async_copy(lens_hbm, lens_in, in_sem.at[4]),
        pltpu.make_async_copy(slot_hbm, slot_in, in_sem.at[5]),
    ]
    for load in loads:
        load.start()

    row_i, col_i = iota((tok, tok), 0), iota((tok, tok), 1)
    swapped = (row_i // peer % nx) * blk + (row_i // blk) * peer + row_i % peer
    regroup = (swapped == col_i).astype(BF16)
    eye = (row_i == col_i).astype(F32)
    eye_low = eye.astype(BF16)

    loads[0].wait()
    s_g0[...] = mm(regroup, in_g[...]).astype(BF16)
    for load in loads[1:]:
        load.wait()
    pl.semaphore_wait(barrier, ny + nx + nz - 2)

    along("y", in_kv, y_kv, a_send.at[0], a_recv.at[0])
    along("y", in_q, y_q, a_send.at[1], a_recv.at[1])
    along("x", s_g0, x_g, a_send.at[2], a_recv.at[2])

    slot = slot_in[...]
    arrived = (slot // peer % nx) * blk + (slot // blk) * peer + slot % peer
    pos_col = jnp.sum(jnp.where(row_i == arrived, col_i.astype(F32), 0.0), axis=1, keepdims=True)
    pos_row = jnp.sum(eye * pos_col, axis=0, keepdims=True)
    lens_pad[...] = jnp.zeros_like(lens_pad)
    lens_pad[:, pl.ds(0, lens_in.shape[1])] = lens_in[...].astype(F32)
    lens = lens_pad[...]
    pad = lens.shape[1]
    below = iota((pad, pad), 1) <= iota((pad, pad), 0)
    ends_col = jnp.sum(jnp.where(below, lens, 0.0), axis=1, keepdims=True)
    first = (ctx * tok).astype(F32)
    doc_row = jnp.sum((ends_col <= pos_row + first).astype(F32), axis=0, keepdims=True)
    doc_col = jnp.sum(eye * doc_row, axis=1, keepdims=True)
    seen = (doc_col == doc_row) & (pos_col <= pos_row)
    own = jnp.where(seen, 0.0, NEG)
    later = jnp.where(lens[:, :1] >= first + tok, 0.0, NEG) + jnp.zeros((tok, tok), F32)
    bias[0, pl.ds(0, tok), :] = jnp.where(core == 0, own, later)
    bias[0, pl.ds(tok, tok), :] = jnp.where(core == 0, NEG, own)
    bias[1, pl.ds(0, tok), :] = later
    bias[1, pl.ds(tok, tok), :] = later
    m_row[...] = jnp.full_like(m_row, NEG)
    l_row[...] = jnp.zeros_like(l_row)
    o_t[...] = jnp.zeros_like(o_t)
    dq_t[...] = jnp.zeros_like(dq_t)

    drain(others(y_kv), a_recv.at[0])
    s_kv[...] = mm(regroup, y_kv[...]).astype(BF16)
    along("x", s_kv, kv_all.at[ctx], b_send.at[0], b_recv.at[0])
    drain(others(x_g), a_recv.at[2])
    s_g[...] = mm(regroup, x_g[...]).astype(BF16)
    along("y", s_g, g_all, b_send.at[2], b_recv.at[2])
    drain(others(y_q), a_recv.at[1])
    s_q[...] = mm(regroup, y_q[...]).astype(BF16)
    along("x", s_q, q_all, b_send.at[1], b_recv.at[1])

    def offset(t):
        return jnp.where(t % 2 == 1, (t + 1) // 2, (nz - t // 2) % nz)

    drain(others(s_kv), b_recv.at[0])

    def to_core(zz):
        here = kv_all.at[zz * 2 + core]
        remote(here, here, fwd_send.at[zz], fwd_recv.at[zz], sibling).start()

    def kv_out(i, carry):
        o = offset(nz - 1 - i)

        @pl.when(z + o < nz)
        def _():
            remote(kv_all.at[ctx], kv_all.at[ctx], z_send.at[z + o], z_recv.at[z], at(y, x, z + o)).start()

        return carry

    lax.fori_loop(0, nz - 1, kv_out, 0)
    to_core(z)

    drain(others(q_all), b_recv.at[1])
    for h in range(heads):
        qf[pl.ds(h * tok, tok), :] = q_all[:, pl.ds(h * dh, dh)]
    drain(others(g_all), b_recv.at[2])
    for h in range(heads):
        grad = mm(regroup, g_all[:, pl.ds(h * dh, dh)]).astype(BF16)
        gf[pl.ds(h * tok, tok), :] = grad
        gt[:, pl.ds(h * tok, tok)] = mm_nt(eye_low, grad)

    def pair(zz):
        both = kv_all[pl.ds(zz * 2, 2)].reshape(2 * tok, 2 * dh)
        return both[:, :dh], both[:, dh:]

    def forward(t, carry):
        o = offset(t)
        nxt = offset(t + 1)

        @pl.when((t + 1 < nz) & (z >= nxt))
        def _():
            drain(s_kv, z_recv.at[z - nxt])
            to_core(z - nxt)

        @pl.when(z >= o)
        def _():
            zz = z - o
            drain(s_kv, fwd_recv.at[zz])
            key, value = pair(zz)
            shift = bias[jnp.minimum(o, 1)]
            score = mm_nt(key, qf[...]) * scale + jnp.concatenate([shift] * heads, axis=1)
            s_all[zz] = score
            dp_all[zz] = mm_nt(value, gf[...])
            old = m_row[...]
            new = jnp.maximum(old, jnp.max(score, axis=0, keepdims=True))
            weight = jnp.exp(score - new)
            fade = jnp.exp(old - new)
            m_row[...] = new
            l_row[...] = l_row[...] * fade + jnp.sum(weight, axis=0, keepdims=True)
            value_t = mm_nt(eye_low, value).astype(BF16)
            o_t[...] = o_t[...] * fade + mm(value_t, weight.astype(BF16))

        return carry

    lax.fori_loop(0, nz, forward, 0)

    attended_t = (o_t[...] * (1.0 / l_row[...])).astype(BF16)
    delta = jnp.sum(gt[...] * attended_t.astype(F32), axis=0, keepdims=True)
    log_total = m_row[...] + jnp.log(l_row[...])

    def send_x(i, value_t):
        for h in range(heads):
            x_out[i, :, pl.ds(h * dh, dh)] = mm_nt(eye_low, value_t[:, h * tok : (h + 1) * tok]).astype(BF16)
        along("x", x_out.at[i], r_out.at[i], xo_send.at[i], xo_recv.at[i])

    def send_y(i, dst):
        drain(others(r_out.at[i]), xo_recv.at[i])
        z_out[i] = mm(regroup, r_out[i]).astype(BF16)
        along("y", z_out.at[i], dst, yo_send.at[i], yo_recv.at[i])

    send_x(0, attended_t)

    def share(zz):
        drain(s_kv, part_recv.at[zz])
        comb[zz] = (part[zz, core].astype(F32) + sib_part[zz].astype(F32)).astype(BF16)
        remote(comb.at[zz], acc.at[z], acc_send.at[zz], acc_recv.at[z], at(y, x, zz)).start()

    def backward(i, carry):
        t = nz - 1 - i
        o = offset(t)
        last = offset(t + 2)

        @pl.when(z >= o)
        def _():
            zz = z - o
            key, value = pair(zz)
            prob = jnp.exp(s_all[zz] - log_total)
            score_grad = (prob * (dp_all[zz] - delta)).astype(BF16)
            key_t = mm_nt(eye_low, key).astype(BF16)
            value_part = mm(prob.astype(BF16), gf[...])
            key_part = mm(score_grad, qf[...]) * scale
            for b in range(2):
                part[zz, b, :, pl.ds(0, dh)] = key_part[b * tok : (b + 1) * tok].astype(BF16)
                part[zz, b, :, pl.ds(dh, dh)] = value_part[b * tok : (b + 1) * tok].astype(BF16)
            remote(part.at[zz, 1 - core], sib_part.at[zz], part_send.at[zz], part_recv.at[zz], sibling).start()
            dq_t[...] += mm(key_t, score_grad)

        @pl.when((t + 2 < nz) & (z >= last))
        def _():
            share(z - last)

        return carry

    lax.fori_loop(0, nz, backward, 0)

    @pl.when(z >= 1)
    def _():
        share(z - 1)

    send_x(1, (dq_t[...] * scale).astype(BF16))
    send_y(0, f_o)

    drain(s_kv, part_recv.at[z])
    total = part[z, core].astype(F32) + sib_part[z].astype(F32)
    for zz in range(nz):

        @pl.when(zz > z)
        def _():
            drain(s_kv, acc_recv.at[zz])

        @pl.when(zz <= z)
        def _():
            acc[zz] = jnp.zeros((tok, 2 * dh), BF16)

        total = total + acc[zz].astype(F32)
    s_dkv[...] = total.astype(BF16)
    along("x", s_dkv, r_dkv, xo_send.at[2], xo_recv.at[2])
    send_y(1, f_dq)
    drain(others(r_dkv), xo_recv.at[2])
    z_dkv[...] = mm(regroup, r_dkv[...]).astype(BF16)
    along("y", z_dkv, f_kv, yo_send.at[2], yo_recv.at[2])

    for i, (first_ref, second_ref) in enumerate(((in_kv, s_kv), (in_q, s_q), (s_g0, s_g))):
        drain(others(first_ref), a_send.at[i])
        drain(others(second_ref), b_send.at[i])
    for zz in range(nz):

        @pl.when(zz > z)
        def _():
            drain(s_kv, z_send.at[zz])

        @pl.when(zz < z)
        def _():
            drain(s_kv, acc_send.at[zz])

        @pl.when(zz <= z)
        def _():
            drain(s_kv, fwd_send.at[zz])
            drain(s_kv, part_send.at[zz])

    for i in range(2):
        drain(others(x_out.at[i]), xo_send.at[i])
        drain(others(z_out.at[i]), yo_send.at[i])
    drain(others(s_dkv), xo_send.at[2])
    drain(others(z_dkv), yo_send.at[2])
    drain(others(f_o), yo_recv.at[0])
    drain(others(f_dq), yo_recv.at[1])
    drain(others(f_kv), yo_recv.at[2])


def write_out(o_in, dq_in, kv_in, o_hbm, dq_hbm, dk_hbm, dv_hbm, sem):
    dh = dk_hbm.shape[1]
    copies = [
        pltpu.make_async_copy(o_in, o_hbm, sem.at[0]),
        pltpu.make_async_copy(dq_in, dq_hbm, sem.at[1]),
        pltpu.make_async_copy(kv_in.at[:, pl.ds(0, dh)], dk_hbm, sem.at[2]),
        pltpu.make_async_copy(kv_in.at[:, pl.ds(dh, dh)], dv_hbm, sem.at[3]),
    ]
    for copy in copies:
        copy.start()
    for copy in copies:
        copy.wait()


def local(ny, nx, nz, queries, keys, values, out_grad, doc_lengths, source_slot):
    tok, dh = keys.shape
    wide = queries.shape[1]
    heads = wide // dh
    flat = heads * tok
    docs = doc_lengths.shape[1]
    pad = -(-docs // 128) * 128
    dma = pltpu.SemaphoreType.DMA
    hbm = pl.BlockSpec(memory_space=pltpu.MemorySpace.HBM)
    vmem = pl.BlockSpec(memory_space=pltpu.VMEM)
    low = lambda *shape: pltpu.VMEM(shape, BF16)
    full = lambda *shape: pltpu.VMEM(shape, F32)
    whole = lambda *shape: pltpu.VMEM(shape, jnp.int32)
    found = pl.pallas_call(
        functools.partial(kernel, ny, nx, nz, heads),
        out_shape=(OUT(tok, wide), OUT(tok, wide), OUT(tok, 2 * dh)),
        in_specs=[hbm] * 6,
        out_specs=[vmem] * 3,
        scratch_shapes=[
            low(tok, 2 * dh), low(tok, wide), low(tok, wide), whole(1, docs), whole(1, tok),
            low(tok, 2 * dh), low(tok, wide), low(tok, wide),
            low(tok, 2 * dh), low(tok, wide), low(tok, wide), low(tok, wide),
            low(2 * nz, tok, 2 * dh), low(tok, wide), low(tok, wide),
            low(flat, dh), low(flat, dh), full(dh, flat),
            full(nz, 2 * tok, flat), full(nz, 2 * tok, flat),
            full(2, 2 * tok, tok), full(1, pad),
            full(1, flat), full(1, flat), full(dh, flat), full(dh, flat),
            low(2, tok, wide), low(2, tok, wide), low(2, tok, wide),
            low(nz, 2, tok, 2 * dh), low(nz, tok, 2 * dh), low(nz, tok, 2 * dh),
            low(nz, tok, 2 * dh), low(tok, 2 * dh), low(tok, 2 * dh), low(tok, 2 * dh),
            dma((6,)), dma((3,)), dma((3,)), dma((3,)), dma((3,)), dma((nz,)), dma((nz,)), dma((nz,)), dma((nz,)),
            dma((3,)), dma((3,)), dma((3,)), dma((3,)), dma((nz,)), dma((nz,)), dma((nz,)), dma((nz,)),
        ],
        compiler_params=pltpu.CompilerParams(collective_id=0, has_side_effects=True),
        name="packed_attention",
    )(queries, keys, values, out_grad, doc_lengths, source_slot.reshape(1, tok))
    shapes = [(tok, wide), (tok, wide), (tok, dh), (tok, dh)]
    return pl.pallas_call(
        write_out,
        out_shape=tuple(jax.ShapeDtypeStruct(shape, BF16) for shape in shapes),
        in_specs=[vmem] * 3,
        out_specs=[hbm] * 4,
        scratch_shapes=[dma((4,))],
        name="write_out",
    )(*[pltpu.with_memory_space_constraint(each, pltpu.VMEM) for each in found])


def solution(mesh):
    side = math.isqrt(mesh.shape["dp"])
    placed = (
        P(("dp", "ctx"), None),
        P(("dp", "ctx"), None),
        P(("dp", "ctx"), None),
        P(("dp", "ctx"), None),
        P("dp", None),
        P(("dp", "ctx")),
    )
    return jax.shard_map(
        functools.partial(local, side, side, mesh.shape["ctx"] // 2),
        mesh=mesh,
        in_specs=placed,
        out_specs=(
            P(("dp", "ctx"), None),
            P(("dp", "ctx"), None),
            P(("dp", "ctx"), None),
            P(("dp", "ctx"), None),
        ),
        check_vma=False,
    )
```

```python
import functools
import math

import jax
import jax.numpy as jnp
from jax import lax
from jax.experimental import pallas as pl
from jax.experimental.pallas import tpu as pltpu
from jax.sharding import PartitionSpec as P

MESH = pl.DeviceIdType.MESH
NEG = -1e30
F32 = jnp.float32
BF16 = jnp.bfloat16


def OUT(*shape):
    return pltpu.VMEM(shape, BF16)


def mm(left, right):
    return jnp.dot(left, right, preferred_element_type=F32)


def mm_nt(left, right):
    return lax.dot_general(left, right, (((1,), (1,)), ((), ())), preferred_element_type=F32)


def iota(shape, dim):
    return lax.broadcasted_iota(jnp.int32, shape, dim)


def far_first(n):
    order = sorted(range(1, n), key=lambda k: -min(k, n - k))
    return order


def kernel(
    ny, nx, nz, heads,
    q_hbm, k_hbm, v_hbm, g_hbm, lens_hbm, slot_hbm,
    f_o, f_dq, f_kv,
    in_kv, in_q, in_g, lens_in, slot_in, y_kv, y_q, x_g, s_kv, s_q, s_g0, s_g, kv_all, q_all, g_all,
    qf, gf, gt, s_all, dp_all, bias, lens_pad, m_row, l_row, o_t, dq_t,
    x_out, r_out, z_out, part, sib_part, comb, acc, s_dkv, r_dkv, z_dkv,
    in_sem, a_send, a_recv, b_send, b_recv, z_send, z_recv, fwd_send, fwd_recv,
    xo_send, xo_recv, yo_send, yo_recv, part_send, part_recv, acc_send, acc_recv,
):
    tok = in_kv.shape[0]
    dh = k_hbm.shape[1]
    wide = heads * dh
    peer = tok // (ny * nx)
    blk = tok // ny
    scale = dh ** -0.5
    dp = lax.axis_index("dp")
    ctx = lax.axis_index("ctx")
    y, x = dp // nx, dp % nx
    z, core = ctx // 2, ctx % 2
    sibling = (dp, z * 2 + 1 - core)

    def at(yy, xx, zz):
        return (yy * nx + xx, zz * 2 + core)

    def rows(i):
        return pl.ds(pl.multiple_of(i * blk, blk), blk)

    def remote(src, dst, send, recv, dev):
        return pltpu.make_async_remote_copy(
            src_ref=src, dst_ref=dst, send_sem=send, recv_sem=recv, device_id=dev, device_id_type=MESH
        )

    def drain(ref, sem):
        pltpu.make_async_copy(ref, ref, sem).wait()

    def others(ref):
        return ref.at[pl.ds(0, tok - blk)]

    def along(axis, src, dst, send, recv):
        me = y if axis == "y" else x
        n = ny if axis == "y" else nx
        for k in far_first(n):
            t = (me + k) % n
            dev = at(t, x, z) if axis == "y" else at(y, t, z)
            remote(src.at[rows(t)], dst.at[rows(me)], send, recv, dev).start()
        dst[rows(me), :] = src[rows(me), :]

    barrier = pltpu.get_barrier_semaphore()
    for k in far_first(ny):
        pl.semaphore_signal(barrier, inc=1, device_id=at((y + k) % ny, x, z), device_id_type=MESH)
    for k in far_first(nx):
        pl.semaphore_signal(barrier, inc=1, device_id=at(y, (x + k) % nx, z), device_id_type=MESH)
    for k in far_first(nz):
        pl.semaphore_signal(barrier, inc=1, device_id=at(y, x, (z + k) % nz), device_id_type=MESH)
    pl.semaphore_signal(barrier, inc=1, device_id=sibling, device_id_type=MESH)

    loads = [
        pltpu.make_async_copy(g_hbm, in_g, in_sem.at[0]),
        pltpu.make_async_copy(k_hbm, in_kv.at[:, pl.ds(0, dh)], in_sem.at[1]),
        pltpu.make_async_copy(v_hbm, in_kv.at[:, pl.ds(dh, dh)], in_sem.at[2]),
        pltpu.make_async_copy(q_hbm, in_q, in_sem.at[3]),
        pltpu.make_async_copy(lens_hbm, lens_in, in_sem.at[4]),
        pltpu.make_async_copy(slot_hbm, slot_in, in_sem.at[5]),
    ]
    for load in loads:
        load.start()

    row_i, col_i = iota((tok, tok), 0), iota((tok, tok), 1)
    swapped = (row_i // peer % nx) * blk + (row_i // blk) * peer + row_i % peer
    regroup = (swapped == col_i).astype(BF16)
    eye = (row_i == col_i).astype(F32)
    eye_low = eye.astype(BF16)

    loads[0].wait()
    s_g0[...] = mm(regroup, in_g[...]).astype(BF16)
    for load in loads[1:]:
        load.wait()
    pl.semaphore_wait(barrier, ny + nx + nz - 2)

    along("y", in_kv, y_kv, a_send.at[0], a_recv.at[0])
    along("y", in_q, y_q, a_send.at[1], a_recv.at[1])
    along("x", s_g0, x_g, a_send.at[2], a_recv.at[2])

    slot = slot_in[...]
    arrived = (slot // peer % nx) * blk + (slot // blk) * peer + slot % peer
    pos_col = jnp.sum(jnp.where(row_i == arrived, col_i.astype(F32), 0.0), axis=1, keepdims=True)
    pos_row = jnp.sum(eye * pos_col, axis=0, keepdims=True)
    lens_pad[...] = jnp.zeros_like(lens_pad)
    lens_pad[:, pl.ds(0, lens_in.shape[1])] = lens_in[...].astype(F32)
    lens = lens_pad[...]
    pad = lens.shape[1]
    below = iota((pad, pad), 1) <= iota((pad, pad), 0)
    ends_col = jnp.sum(jnp.where(below, lens, 0.0), axis=1, keepdims=True)
    first = (ctx * tok).astype(F32)
    doc_row = jnp.sum((ends_col <= pos_row + first).astype(F32), axis=0, keepdims=True)
    doc_col = jnp.sum(eye * doc_row, axis=1, keepdims=True)
    seen = (doc_col == doc_row) & (pos_col <= pos_row)
    own = jnp.where(seen, 0.0, NEG)
    later = jnp.where(lens[:, :1] >= first + tok, 0.0, NEG) + jnp.zeros((tok, tok), F32)
    bias[0, pl.ds(0, tok), :] = jnp.where(core == 0, own, later)
    bias[0, pl.ds(tok, tok), :] = jnp.where(core == 0, NEG, own)
    bias[1, pl.ds(0, tok), :] = later
    bias[1, pl.ds(tok, tok), :] = later
    m_row[...] = jnp.full_like(m_row, NEG)
    l_row[...] = jnp.zeros_like(l_row)
    o_t[...] = jnp.zeros_like(o_t)
    dq_t[...] = jnp.zeros_like(dq_t)

    drain(others(y_kv), a_recv.at[0])
    s_kv[...] = mm(regroup, y_kv[...]).astype(BF16)
    along("x", s_kv, kv_all.at[ctx], b_send.at[0], b_recv.at[0])
    drain(others(x_g), a_recv.at[2])
    s_g[...] = mm(regroup, x_g[...]).astype(BF16)
    along("y", s_g, g_all, b_send.at[2], b_recv.at[2])
    drain(others(y_q), a_recv.at[1])
    s_q[...] = mm(regroup, y_q[...]).astype(BF16)
    along("x", s_q, q_all, b_send.at[1], b_recv.at[1])

    def offset(t):
        return jnp.where(t % 2 == 1, (t + 1) // 2, (nz - t // 2) % nz)

    drain(others(s_kv), b_recv.at[0])

    def to_core(zz):
        here = kv_all.at[zz * 2 + core]
        remote(here, here, fwd_send.at[zz], fwd_recv.at[zz], sibling).start()

    def kv_out(i, carry):
        o = i + 1

        @pl.when(z + o < nz)
        def _():
            remote(kv_all.at[ctx], kv_all.at[ctx], z_send.at[z + o], z_recv.at[z], at(y, x, z + o)).start()

        return carry

    lax.fori_loop(0, nz - 1, kv_out, 0)
    to_core(z)

    drain(others(q_all), b_recv.at[1])
    for h in range(heads):
        qf[pl.ds(h * tok, tok), :] = q_all[:, pl.ds(h * dh, dh)]
    drain(others(g_all), b_recv.at[2])
    for h in range(heads):
        grad = mm(regroup, g_all[:, pl.ds(h * dh, dh)]).astype(BF16)
        gf[pl.ds(h * tok, tok), :] = grad
        gt[:, pl.ds(h * tok, tok)] = mm_nt(eye_low, grad)

    def pair(zz):
        both = kv_all[pl.ds(zz * 2, 2)].reshape(2 * tok, 2 * dh)
        return both[:, :dh], both[:, dh:]

    def forward(t, carry):
        o = t
        nxt = t + 1

        @pl.when((t + 1 < nz) & (z >= nxt))
        def _():
            drain(s_kv, z_recv.at[z - nxt])
            to_core(z - nxt)

        @pl.when(z >= o)
        def _():
            zz = z - o
            drain(s_kv, fwd_recv.at[zz])
            key, value = pair(zz)
            shift = bias[jnp.minimum(o, 1)]
            score = mm_nt(key, qf[...]) * scale + jnp.concatenate([shift] * heads, axis=1)
            s_all[zz] = score
            dp_all[zz] = mm_nt(value, gf[...])
            old = m_row[...]
            new = jnp.maximum(old, jnp.max(score, axis=0, keepdims=True))
            weight = jnp.exp(score - new)
            fade = jnp.exp(old - new)
            m_row[...] = new
            l_row[...] = l_row[...] * fade + jnp.sum(weight, axis=0, keepdims=True)
            value_t = mm_nt(eye_low, value).astype(BF16)
            o_t[...] = o_t[...] * fade + mm(value_t, weight.astype(BF16))

        return carry

    lax.fori_loop(0, nz, forward, 0)

    attended_t = (o_t[...] * (1.0 / l_row[...])).astype(BF16)
    delta = jnp.sum(gt[...] * attended_t.astype(F32), axis=0, keepdims=True)
    log_total = m_row[...] + jnp.log(l_row[...])

    def send_x(i, value_t):
        for h in range(heads):
            x_out[i, :, pl.ds(h * dh, dh)] = mm_nt(eye_low, value_t[:, h * tok : (h + 1) * tok]).astype(BF16)
        along("x", x_out.at[i], r_out.at[i], xo_send.at[i], xo_recv.at[i])

    def send_y(i, dst):
        drain(others(r_out.at[i]), xo_recv.at[i])
        z_out[i] = mm(regroup, r_out[i]).astype(BF16)
        along("y", z_out.at[i], dst, yo_send.at[i], yo_recv.at[i])

    send_x(0, attended_t)

    def share(zz):
        drain(s_kv, part_recv.at[zz])
        comb[zz] = (part[zz, core].astype(F32) + sib_part[zz].astype(F32)).astype(BF16)
        remote(comb.at[zz], acc.at[z], acc_send.at[zz], acc_recv.at[z], at(y, x, zz)).start()

    def backward(i, carry):
        t = nz - 1 - i
        o = offset(t)
        last = offset(t + 2)

        @pl.when(z >= o)
        def _():
            zz = z - o
            key, value = pair(zz)
            prob = jnp.exp(s_all[zz] - log_total)
            score_grad = (prob * (dp_all[zz] - delta)).astype(BF16)
            key_t = mm_nt(eye_low, key).astype(BF16)
            value_part = mm(prob.astype(BF16), gf[...])
            key_part = mm(score_grad, qf[...]) * scale
            for b in range(2):
                part[zz, b, :, pl.ds(0, dh)] = key_part[b * tok : (b + 1) * tok].astype(BF16)
                part[zz, b, :, pl.ds(dh, dh)] = value_part[b * tok : (b + 1) * tok].astype(BF16)
            remote(part.at[zz, 1 - core], sib_part.at[zz], part_send.at[zz], part_recv.at[zz], sibling).start()
            dq_t[...] += mm(key_t, score_grad)

        @pl.when((t + 2 < nz) & (z >= last))
        def _():
            share(z - last)

        return carry

    lax.fori_loop(0, nz, backward, 0)

    @pl.when(z >= 1)
    def _():
        share(z - 1)

    send_x(1, (dq_t[...] * scale).astype(BF16))
    send_y(0, f_o)

    drain(s_kv, part_recv.at[z])
    total = part[z, core].astype(F32) + sib_part[z].astype(F32)
    for zz in range(nz):

        @pl.when(zz > z)
        def _():
            drain(s_kv, acc_recv.at[zz])

        @pl.when(zz <= z)
        def _():
            acc[zz] = jnp.zeros((tok, 2 * dh), BF16)

        total = total + acc[zz].astype(F32)
    s_dkv[...] = total.astype(BF16)
    along("x", s_dkv, r_dkv, xo_send.at[2], xo_recv.at[2])
    send_y(1, f_dq)
    drain(others(r_dkv), xo_recv.at[2])
    z_dkv[...] = mm(regroup, r_dkv[...]).astype(BF16)
    along("y", z_dkv, f_kv, yo_send.at[2], yo_recv.at[2])

    for i, (first_ref, second_ref) in enumerate(((in_kv, s_kv), (in_q, s_q), (s_g0, s_g))):
        drain(others(first_ref), a_send.at[i])
        drain(others(second_ref), b_send.at[i])
    for zz in range(nz):

        @pl.when(zz > z)
        def _():
            drain(s_kv, z_send.at[zz])

        @pl.when(zz < z)
        def _():
            drain(s_kv, acc_send.at[zz])

        @pl.when(zz <= z)
        def _():
            drain(s_kv, fwd_send.at[zz])
            drain(s_kv, part_send.at[zz])

    for i in range(2):
        drain(others(x_out.at[i]), xo_send.at[i])
        drain(others(z_out.at[i]), yo_send.at[i])
    drain(others(s_dkv), xo_send.at[2])
    drain(others(z_dkv), yo_send.at[2])
    drain(others(f_o), yo_recv.at[0])
    drain(others(f_dq), yo_recv.at[1])
    drain(others(f_kv), yo_recv.at[2])


def write_out(o_in, dq_in, kv_in, o_hbm, dq_hbm, dk_hbm, dv_hbm, sem):
    dh = dk_hbm.shape[1]
    copies = [
        pltpu.make_async_copy(o_in, o_hbm, sem.at[0]),
        pltpu.make_async_copy(dq_in, dq_hbm, sem.at[1]),
        pltpu.make_async_copy(kv_in.at[:, pl.ds(0, dh)], dk_hbm, sem.at[2]),
        pltpu.make_async_copy(kv_in.at[:, pl.ds(dh, dh)], dv_hbm, sem.at[3]),
    ]
    for copy in copies:
        copy.start()
    for copy in copies:
        copy.wait()


def local(ny, nx, nz, queries, keys, values, out_grad, doc_lengths, source_slot):
    tok, dh = keys.shape
    wide = queries.shape[1]
    heads = wide // dh
    flat = heads * tok
    docs = doc_lengths.shape[1]
    pad = -(-docs // 128) * 128
    dma = pltpu.SemaphoreType.DMA
    hbm = pl.BlockSpec(memory_space=pltpu.MemorySpace.HBM)
    vmem = pl.BlockSpec(memory_space=pltpu.VMEM)
    low = lambda *shape: pltpu.VMEM(shape, BF16)
    full = lambda *shape: pltpu.VMEM(shape, F32)
    whole = lambda *shape: pltpu.VMEM(shape, jnp.int32)
    found = pl.pallas_call(
        functools.partial(kernel, ny, nx, nz, heads),
        out_shape=(OUT(tok, wide), OUT(tok, wide), OUT(tok, 2 * dh)),
        in_specs=[hbm] * 6,
        out_specs=[vmem] * 3,
        scratch_shapes=[
            low(tok, 2 * dh), low(tok, wide), low(tok, wide), whole(1, docs), whole(1, tok),
            low(tok, 2 * dh), low(tok, wide), low(tok, wide),
            low(tok, 2 * dh), low(tok, wide), low(tok, wide), low(tok, wide),
            low(2 * nz, tok, 2 * dh), low(tok, wide), low(tok, wide),
            low(flat, dh), low(flat, dh), full(dh, flat),
            full(nz, 2 * tok, flat), full(nz, 2 * tok, flat),
            full(2, 2 * tok, tok), full(1, pad),
            full(1, flat), full(1, flat), full(dh, flat), full(dh, flat),
            low(2, tok, wide), low(2, tok, wide), low(2, tok, wide),
            low(nz, 2, tok, 2 * dh), low(nz, tok, 2 * dh), low(nz, tok, 2 * dh),
            low(nz, tok, 2 * dh), low(tok, 2 * dh), low(tok, 2 * dh), low(tok, 2 * dh),
            dma((6,)), dma((3,)), dma((3,)), dma((3,)), dma((3,)), dma((nz,)), dma((nz,)), dma((nz,)), dma((nz,)),
            dma((3,)), dma((3,)), dma((3,)), dma((3,)), dma((nz,)), dma((nz,)), dma((nz,)), dma((nz,)),
        ],
        compiler_params=pltpu.CompilerParams(collective_id=0, has_side_effects=True),
        name="packed_attention",
    )(queries, keys, values, out_grad, doc_lengths, source_slot.reshape(1, tok))
    shapes = [(tok, wide), (tok, wide), (tok, dh), (tok, dh)]
    return pl.pallas_call(
        write_out,
        out_shape=tuple(jax.ShapeDtypeStruct(shape, BF16) for shape in shapes),
        in_specs=[vmem] * 3,
        out_specs=[hbm] * 4,
        scratch_shapes=[dma((4,))],
        name="write_out",
    )(*[pltpu.with_memory_space_constraint(each, pltpu.VMEM) for each in found])


def solution(mesh):
    side = math.isqrt(mesh.shape["dp"])
    placed = (
        P(("dp", "ctx"), None),
        P(("dp", "ctx"), None),
        P(("dp", "ctx"), None),
        P(("dp", "ctx"), None),
        P("dp", None),
        P(("dp", "ctx")),
    )
    return jax.shard_map(
        functools.partial(local, side, side, mesh.shape["ctx"] // 2),
        mesh=mesh,
        in_specs=placed,
        out_specs=(
            P(("dp", "ctx"), None),
            P(("dp", "ctx"), None),
            P(("dp", "ctx"), None),
            P(("dp", "ctx"), None),
        ),
        check_vma=False,
    )
```

```python
import functools
import math

import jax
import jax.numpy as jnp
from jax import lax
from jax.experimental import pallas as pl
from jax.experimental.pallas import tpu as pltpu
from jax.sharding import PartitionSpec as P

MESH = pl.DeviceIdType.MESH
NEG = -1e30
F32 = jnp.float32
BF16 = jnp.bfloat16


def OUT(*shape):
    return pltpu.VMEM(shape, BF16)


def mm(left, right):
    return jnp.dot(left, right, preferred_element_type=F32)


def mm_nt(left, right):
    return lax.dot_general(left, right, (((1,), (1,)), ((), ())), preferred_element_type=F32)


def iota(shape, dim):
    return lax.broadcasted_iota(jnp.int32, shape, dim)


def far_first(n):
    order = sorted(range(1, n), key=lambda k: -min(k, n - k))
    return order


def kernel(
    ny, nx, nz, heads,
    q_hbm, k_hbm, v_hbm, g_hbm, lens_hbm, slot_hbm,
    f_o, f_dq, f_kv,
    in_kv, in_q, in_g, lens_in, slot_in, y_kv, y_q, x_g, s_kv, s_q, s_g0, s_g, kv_all, q_all, g_all,
    qf, gf, gt, s_all, dp_all, bias, lens_pad, m_row, l_row, o_t, dq_t,
    x_out, r_out, z_out, part, sib_part, comb, acc, s_dkv, r_dkv, z_dkv,
    in_sem, a_send, a_recv, b_send, b_recv, z_send, z_recv, fwd_send, fwd_recv,
    xo_send, xo_recv, yo_send, yo_recv, part_send, part_recv, acc_send, acc_recv,
    ready,
):
    tok = in_kv.shape[0]
    dh = k_hbm.shape[1]
    wide = heads * dh
    peer = tok // (ny * nx)
    blk = tok // ny
    scale = dh ** -0.5
    dp = lax.axis_index("dp")
    ctx = lax.axis_index("ctx")
    y, x = dp // nx, dp % nx
    z, core = ctx // 2, ctx % 2
    sibling = (dp, z * 2 + 1 - core)

    def at(yy, xx, zz):
        return (yy * nx + xx, zz * 2 + core)

    def rows(i):
        return pl.ds(pl.multiple_of(i * blk, blk), blk)

    def remote(src, dst, send, recv, dev):
        return pltpu.make_async_remote_copy(
            src_ref=src, dst_ref=dst, send_sem=send, recv_sem=recv, device_id=dev, device_id_type=MESH
        )

    def drain(ref, sem):
        pltpu.make_async_copy(ref, ref, sem).wait()

    def others(ref):
        return ref.at[pl.ds(0, tok - blk)]

    def along(axis, src, dst, send, recv):
        me = y if axis == "y" else x
        n = ny if axis == "y" else nx
        for k in far_first(n):
            t = (me + k) % n
            dev = at(t, x, z) if axis == "y" else at(y, t, z)
            remote(src.at[rows(t)], dst.at[rows(me)], send, recv, dev).start()
        dst[rows(me), :] = src[rows(me), :]

    barrier = pltpu.get_barrier_semaphore()
    for k in far_first(ny):
        pl.semaphore_signal(barrier, inc=1, device_id=at((y + k) % ny, x, z), device_id_type=MESH)
    for k in far_first(nx):
        pl.semaphore_signal(barrier, inc=1, device_id=at(y, (x + k) % nx, z), device_id_type=MESH)
    pl.semaphore_signal(barrier, inc=1, device_id=sibling, device_id_type=MESH)
    late_line = (dp == 0) & (core == 0)
    late = late_line & (z == 0)
    for zz in range(1, nz):

        @pl.when((zz > z) & jnp.logical_not(late))
        def _():
            pl.semaphore_signal(barrier, inc=1, device_id=at(y, x, zz), device_id_type=MESH)

    @pl.when(late_line & (z > 0))
    def _():
        pl.semaphore_signal(barrier, inc=1, device_id=at(y, x, 0), device_id_type=MESH)

    from_z = jnp.where(late, nz - 1, jnp.where(late_line, z - 1, z))

    loads = [
        pltpu.make_async_copy(g_hbm, in_g, in_sem.at[0]),
        pltpu.make_async_copy(k_hbm, in_kv.at[:, pl.ds(0, dh)], in_sem.at[1]),
        pltpu.make_async_copy(v_hbm, in_kv.at[:, pl.ds(dh, dh)], in_sem.at[2]),
        pltpu.make_async_copy(q_hbm, in_q, in_sem.at[3]),
        pltpu.make_async_copy(lens_hbm, lens_in, in_sem.at[4]),
        pltpu.make_async_copy(slot_hbm, slot_in, in_sem.at[5]),
    ]
    for load in loads:
        load.start()

    row_i, col_i = iota((tok, tok), 0), iota((tok, tok), 1)
    swapped = (row_i // peer % nx) * blk + (row_i // blk) * peer + row_i % peer
    regroup = (swapped == col_i).astype(BF16)
    eye = (row_i == col_i).astype(F32)
    eye_low = eye.astype(BF16)

    loads[0].wait()
    s_g0[...] = mm(regroup, in_g[...]).astype(BF16)
    for load in loads[1:]:
        load.wait()
    pl.semaphore_wait(barrier, ny + nx - 1 + from_z)
    for zz in range(nz - 1):

        @pl.when((zz < z) & jnp.logical_not(late_line & (zz == 0)))
        def _():
            pl.semaphore_signal(ready, inc=1, device_id=at(y, x, zz), device_id_type=MESH)


    along("y", in_kv, y_kv, a_send.at[0], a_recv.at[0])
    along("y", in_q, y_q, a_send.at[1], a_recv.at[1])
    along("x", s_g0, x_g, a_send.at[2], a_recv.at[2])

    slot = slot_in[...]
    arrived = (slot // peer % nx) * blk + (slot // blk) * peer + slot % peer
    pos_col = jnp.sum(jnp.where(row_i == arrived, col_i.astype(F32), 0.0), axis=1, keepdims=True)
    pos_row = jnp.sum(eye * pos_col, axis=0, keepdims=True)
    lens_pad[...] = jnp.zeros_like(lens_pad)
    lens_pad[:, pl.ds(0, lens_in.shape[1])] = lens_in[...].astype(F32)
    lens = lens_pad[...]
    pad = lens.shape[1]
    below = iota((pad, pad), 1) <= iota((pad, pad), 0)
    ends_col = jnp.sum(jnp.where(below, lens, 0.0), axis=1, keepdims=True)
    first = (ctx * tok).astype(F32)
    doc_row = jnp.sum((ends_col <= pos_row + first).astype(F32), axis=0, keepdims=True)
    doc_col = jnp.sum(eye * doc_row, axis=1, keepdims=True)
    seen = (doc_col == doc_row) & (pos_col <= pos_row)
    own = jnp.where(seen, 0.0, NEG)
    later = jnp.where(lens[:, :1] >= first + tok, 0.0, NEG) + jnp.zeros((tok, tok), F32)
    bias[0, pl.ds(0, tok), :] = jnp.where(core == 0, own, later)
    bias[0, pl.ds(tok, tok), :] = jnp.where(core == 0, NEG, own)
    bias[1, pl.ds(0, tok), :] = later
    bias[1, pl.ds(tok, tok), :] = later
    m_row[...] = jnp.full_like(m_row, NEG)
    l_row[...] = jnp.zeros_like(l_row)
    o_t[...] = jnp.zeros_like(o_t)
    dq_t[...] = jnp.zeros_like(dq_t)

    drain(others(y_kv), a_recv.at[0])
    s_kv[...] = mm(regroup, y_kv[...]).astype(BF16)
    along("x", s_kv, kv_all.at[ctx], b_send.at[0], b_recv.at[0])
    drain(others(x_g), a_recv.at[2])
    s_g[...] = mm(regroup, x_g[...]).astype(BF16)
    along("y", s_g, g_all, b_send.at[2], b_recv.at[2])
    drain(others(y_q), a_recv.at[1])
    s_q[...] = mm(regroup, y_q[...]).astype(BF16)
    along("x", s_q, q_all, b_send.at[1], b_recv.at[1])

    def offset(t):
        return jnp.where(t % 2 == 1, (t + 1) // 2, (nz - t // 2) % nz)

    drain(others(s_kv), b_recv.at[0])

    def to_core(zz):
        here = kv_all.at[zz * 2 + core]
        remote(here, here, fwd_send.at[zz], fwd_recv.at[zz], sibling).start()

    @pl.when(jnp.logical_not(late) & (z < nz - 1))
    def _():
        pl.semaphore_wait(ready, nz - 1 - z)

    def kv_out(i, carry):
        o = i + 1

        @pl.when(z + o < nz)
        def _():
            remote(kv_all.at[ctx], kv_all.at[ctx], z_send.at[z + o], z_recv.at[z], at(y, x, z + o)).start()

        return carry

    lax.fori_loop(0, nz - 1, kv_out, 0)
    to_core(z)

    drain(others(q_all), b_recv.at[1])
    for h in range(heads):
        qf[pl.ds(h * tok, tok), :] = q_all[:, pl.ds(h * dh, dh)]
    drain(others(g_all), b_recv.at[2])
    for h in range(heads):
        grad = mm(regroup, g_all[:, pl.ds(h * dh, dh)]).astype(BF16)
        gf[pl.ds(h * tok, tok), :] = grad
        gt[:, pl.ds(h * tok, tok)] = mm_nt(eye_low, grad)

    def pair(zz):
        both = kv_all[pl.ds(zz * 2, 2)].reshape(2 * tok, 2 * dh)
        return both[:, :dh], both[:, dh:]

    def forward(t, carry):
        o = t
        nxt = t + 1

        @pl.when((t + 1 < nz) & (z >= nxt))
        def _():
            drain(s_kv, z_recv.at[z - nxt])
            to_core(z - nxt)

        @pl.when(z >= o)
        def _():
            zz = z - o
            drain(s_kv, fwd_recv.at[zz])
            key, value = pair(zz)
            shift = bias[jnp.minimum(o, 1)]
            score = mm_nt(key, qf[...]) * scale + jnp.concatenate([shift] * heads, axis=1)
            s_all[zz] = score
            dp_all[zz] = mm_nt(value, gf[...])
            old = m_row[...]
            new = jnp.maximum(old, jnp.max(score, axis=0, keepdims=True))
            weight = jnp.exp(score - new)
            fade = jnp.exp(old - new)
            m_row[...] = new
            l_row[...] = l_row[...] * fade + jnp.sum(weight, axis=0, keepdims=True)
            value_t = mm_nt(eye_low, value).astype(BF16)
            o_t[...] = o_t[...] * fade + mm(value_t, weight.astype(BF16))

        return carry

    lax.fori_loop(0, nz, forward, 0)

    attended_t = (o_t[...] * (1.0 / l_row[...])).astype(BF16)
    delta = jnp.sum(gt[...] * attended_t.astype(F32), axis=0, keepdims=True)
    log_total = m_row[...] + jnp.log(l_row[...])

    def send_x(i, value_t):
        for h in range(heads):
            x_out[i, :, pl.ds(h * dh, dh)] = mm_nt(eye_low, value_t[:, h * tok : (h + 1) * tok]).astype(BF16)
        along("x", x_out.at[i], r_out.at[i], xo_send.at[i], xo_recv.at[i])

    def send_y(i, dst):
        drain(others(r_out.at[i]), xo_recv.at[i])
        z_out[i] = mm(regroup, r_out[i]).astype(BF16)
        along("y", z_out.at[i], dst, yo_send.at[i], yo_recv.at[i])

    send_x(0, attended_t)

    def share(zz):
        drain(s_kv, part_recv.at[zz])
        comb[zz] = (part[zz, core].astype(F32) + sib_part[zz].astype(F32)).astype(BF16)
        remote(comb.at[zz], acc.at[z], acc_send.at[zz], acc_recv.at[z], at(y, x, zz)).start()

    def backward(i, carry):
        t = nz - 1 - i
        o = offset(t)
        last = offset(t + 2)

        @pl.when(z >= o)
        def _():
            zz = z - o
            key, value = pair(zz)
            prob = jnp.exp(s_all[zz] - log_total)
            score_grad = (prob * (dp_all[zz] - delta)).astype(BF16)
            key_t = mm_nt(eye_low, key).astype(BF16)
            value_part = mm(prob.astype(BF16), gf[...])
            key_part = mm(score_grad, qf[...]) * scale
            for b in range(2):
                part[zz, b, :, pl.ds(0, dh)] = key_part[b * tok : (b + 1) * tok].astype(BF16)
                part[zz, b, :, pl.ds(dh, dh)] = value_part[b * tok : (b + 1) * tok].astype(BF16)
            remote(part.at[zz, 1 - core], sib_part.at[zz], part_send.at[zz], part_recv.at[zz], sibling).start()
            dq_t[...] += mm(key_t, score_grad)

        @pl.when((t + 2 < nz) & (z >= last))
        def _():
            share(z - last)

        return carry

    lax.fori_loop(0, nz, backward, 0)

    @pl.when(z >= 1)
    def _():
        share(z - 1)

    send_x(1, (dq_t[...] * scale).astype(BF16))
    send_y(0, f_o)

    drain(s_kv, part_recv.at[z])
    total = part[z, core].astype(F32) + sib_part[z].astype(F32)
    for zz in range(nz):

        @pl.when(zz > z)
        def _():
            drain(s_kv, acc_recv.at[zz])

        @pl.when(zz <= z)
        def _():
            acc[zz] = jnp.zeros((tok, 2 * dh), BF16)

        total = total + acc[zz].astype(F32)
    s_dkv[...] = total.astype(BF16)
    along("x", s_dkv, r_dkv, xo_send.at[2], xo_recv.at[2])
    send_y(1, f_dq)
    drain(others(r_dkv), xo_recv.at[2])
    z_dkv[...] = mm(regroup, r_dkv[...]).astype(BF16)
    along("y", z_dkv, f_kv, yo_send.at[2], yo_recv.at[2])

    for i, (first_ref, second_ref) in enumerate(((in_kv, s_kv), (in_q, s_q), (s_g0, s_g))):
        drain(others(first_ref), a_send.at[i])
        drain(others(second_ref), b_send.at[i])
    for zz in range(nz):

        @pl.when(zz > z)
        def _():
            drain(s_kv, z_send.at[zz])

        @pl.when(zz < z)
        def _():
            drain(s_kv, acc_send.at[zz])

        @pl.when(zz <= z)
        def _():
            drain(s_kv, fwd_send.at[zz])
            drain(s_kv, part_send.at[zz])

    for i in range(2):
        drain(others(x_out.at[i]), xo_send.at[i])
        drain(others(z_out.at[i]), yo_send.at[i])
    drain(others(s_dkv), xo_send.at[2])
    drain(others(z_dkv), yo_send.at[2])
    drain(others(f_o), yo_recv.at[0])
    drain(others(f_dq), yo_recv.at[1])
    drain(others(f_kv), yo_recv.at[2])


def write_out(o_in, dq_in, kv_in, o_hbm, dq_hbm, dk_hbm, dv_hbm, sem):
    dh = dk_hbm.shape[1]
    copies = [
        pltpu.make_async_copy(o_in, o_hbm, sem.at[0]),
        pltpu.make_async_copy(dq_in, dq_hbm, sem.at[1]),
        pltpu.make_async_copy(kv_in.at[:, pl.ds(0, dh)], dk_hbm, sem.at[2]),
        pltpu.make_async_copy(kv_in.at[:, pl.ds(dh, dh)], dv_hbm, sem.at[3]),
    ]
    for copy in copies:
        copy.start()
    for copy in copies:
        copy.wait()


def local(ny, nx, nz, queries, keys, values, out_grad, doc_lengths, source_slot):
    tok, dh = keys.shape
    wide = queries.shape[1]
    heads = wide // dh
    flat = heads * tok
    docs = doc_lengths.shape[1]
    pad = -(-docs // 128) * 128
    dma = pltpu.SemaphoreType.DMA
    hbm = pl.BlockSpec(memory_space=pltpu.MemorySpace.HBM)
    vmem = pl.BlockSpec(memory_space=pltpu.VMEM)
    low = lambda *shape: pltpu.VMEM(shape, BF16)
    full = lambda *shape: pltpu.VMEM(shape, F32)
    whole = lambda *shape: pltpu.VMEM(shape, jnp.int32)
    found = pl.pallas_call(
        functools.partial(kernel, ny, nx, nz, heads),
        out_shape=(OUT(tok, wide), OUT(tok, wide), OUT(tok, 2 * dh)),
        in_specs=[hbm] * 6,
        out_specs=[vmem] * 3,
        scratch_shapes=[
            low(tok, 2 * dh), low(tok, wide), low(tok, wide), whole(1, docs), whole(1, tok),
            low(tok, 2 * dh), low(tok, wide), low(tok, wide),
            low(tok, 2 * dh), low(tok, wide), low(tok, wide), low(tok, wide),
            low(2 * nz, tok, 2 * dh), low(tok, wide), low(tok, wide),
            low(flat, dh), low(flat, dh), full(dh, flat),
            full(nz, 2 * tok, flat), full(nz, 2 * tok, flat),
            full(2, 2 * tok, tok), full(1, pad),
            full(1, flat), full(1, flat), full(dh, flat), full(dh, flat),
            low(2, tok, wide), low(2, tok, wide), low(2, tok, wide),
            low(nz, 2, tok, 2 * dh), low(nz, tok, 2 * dh), low(nz, tok, 2 * dh),
            low(nz, tok, 2 * dh), low(tok, 2 * dh), low(tok, 2 * dh), low(tok, 2 * dh),
            dma((6,)), dma((3,)), dma((3,)), dma((3,)), dma((3,)), dma((nz,)), dma((nz,)), dma((nz,)), dma((nz,)),
            dma((3,)), dma((3,)), dma((3,)), dma((3,)), dma((nz,)), dma((nz,)), dma((nz,)), dma((nz,)),
            pltpu.SemaphoreType.REGULAR,
        ],
        compiler_params=pltpu.CompilerParams(collective_id=0, has_side_effects=True),
        name="packed_attention",
    )(queries, keys, values, out_grad, doc_lengths, source_slot.reshape(1, tok))
    shapes = [(tok, wide), (tok, wide), (tok, dh), (tok, dh)]
    return pl.pallas_call(
        write_out,
        out_shape=tuple(jax.ShapeDtypeStruct(shape, BF16) for shape in shapes),
        in_specs=[vmem] * 3,
        out_specs=[hbm] * 4,
        scratch_shapes=[dma((4,))],
        name="write_out",
    )(*[pltpu.with_memory_space_constraint(each, pltpu.VMEM) for each in found])


def solution(mesh):
    side = math.isqrt(mesh.shape["dp"])
    placed = (
        P(("dp", "ctx"), None),
        P(("dp", "ctx"), None),
        P(("dp", "ctx"), None),
        P(("dp", "ctx"), None),
        P("dp", None),
        P(("dp", "ctx")),
    )
    return jax.shard_map(
        functools.partial(local, side, side, mesh.shape["ctx"] // 2),
        mesh=mesh,
        in_specs=placed,
        out_specs=(
            P(("dp", "ctx"), None),
            P(("dp", "ctx"), None),
            P(("dp", "ctx"), None),
            P(("dp", "ctx"), None),
        ),
        check_vma=False,
    )
```

```python
import functools
import math

import jax
import jax.numpy as jnp
from jax import lax
from jax.experimental import pallas as pl
from jax.experimental.pallas import tpu as pltpu
from jax.sharding import PartitionSpec as P

MESH = pl.DeviceIdType.MESH
NEG = -1e30
F32 = jnp.float32
BF16 = jnp.bfloat16


def OUT(*shape):
    return pltpu.VMEM(shape, BF16)


def mm(left, right):
    return jnp.dot(left, right, preferred_element_type=F32)


def mm_nt(left, right):
    return lax.dot_general(left, right, (((1,), (1,)), ((), ())), preferred_element_type=F32)


def iota(shape, dim):
    return lax.broadcasted_iota(jnp.int32, shape, dim)


def far_first(n):
    order = sorted(range(1, n), key=lambda k: -min(k, n - k))
    return order


def kernel(
    ny, nx, nz, heads,
    q_hbm, k_hbm, v_hbm, g_hbm, lens_hbm, slot_hbm,
    f_o, f_dq, f_kv,
    in_kv, in_q, in_g, lens_in, slot_in, y_kv, y_q, x_g, s_kv, s_q, s_g0, s_g, kv_all, q_all, g_all,
    qf, gf, gt, s_all, dp_all, bias, lens_pad, m_row, l_row, o_t, dq_t,
    x_out, r_out, z_out, part, sib_part, comb, acc, s_dkv, r_dkv, z_dkv,
    in_sem, a_send, a_recv, b_send, b_recv, z_send, z_recv, fwd_send, fwd_recv,
    xo_send, xo_recv, yo_send, yo_recv, part_send, part_recv, acc_send, acc_recv,
    ready,
):
    tok = in_kv.shape[0]
    dh = k_hbm.shape[1]
    wide = heads * dh
    peer = tok // (ny * nx)
    blk = tok // ny
    scale = dh ** -0.5
    dp = lax.axis_index("dp")
    ctx = lax.axis_index("ctx")
    y, x = dp // nx, dp % nx
    z, core = ctx // 2, ctx % 2
    sibling = (dp, z * 2 + 1 - core)

    def at(yy, xx, zz):
        return (yy * nx + xx, zz * 2 + core)

    def rows(i):
        return pl.ds(pl.multiple_of(i * blk, blk), blk)

    def remote(src, dst, send, recv, dev):
        return pltpu.make_async_remote_copy(
            src_ref=src, dst_ref=dst, send_sem=send, recv_sem=recv, device_id=dev, device_id_type=MESH
        )

    def drain(ref, sem):
        pltpu.make_async_copy(ref, ref, sem).wait()

    def others(ref):
        return ref.at[pl.ds(0, tok - blk)]

    def along(axis, src, dst, send, recv):
        me = y if axis == "y" else x
        n = ny if axis == "y" else nx
        for k in far_first(n):
            t = (me + k) % n
            dev = at(t, x, z) if axis == "y" else at(y, t, z)
            remote(src.at[rows(t)], dst.at[rows(me)], send, recv, dev).start()
        dst[rows(me), :] = src[rows(me), :]

    barrier = pltpu.get_barrier_semaphore()
    for k in far_first(ny):
        pl.semaphore_signal(barrier, inc=1, device_id=at((y + k) % ny, x, z), device_id_type=MESH)
    for k in far_first(nx):
        pl.semaphore_signal(barrier, inc=1, device_id=at(y, (x + k) % nx, z), device_id_type=MESH)
    pl.semaphore_signal(barrier, inc=1, device_id=sibling, device_id_type=MESH)
    late_line = (dp == 0) & (core == 0)
    late = late_line & (z == 0)
    for zz in range(1, nz):

        @pl.when((zz > z) & jnp.logical_not(late))
        def _():
            pl.semaphore_signal(barrier, inc=1, device_id=at(y, x, zz), device_id_type=MESH)

    @pl.when(late_line & (z > 0))
    def _():
        pl.semaphore_signal(barrier, inc=1, device_id=at(y, x, 0), device_id_type=MESH)

    from_z = jnp.where(late, nz - 1, jnp.where(late_line, z - 1, z))

    loads = [
        pltpu.make_async_copy(g_hbm, in_g, in_sem.at[0]),
        pltpu.make_async_copy(k_hbm, in_kv.at[:, pl.ds(0, dh)], in_sem.at[1]),
        pltpu.make_async_copy(v_hbm, in_kv.at[:, pl.ds(dh, dh)], in_sem.at[2]),
        pltpu.make_async_copy(q_hbm, in_q, in_sem.at[3]),
        pltpu.make_async_copy(lens_hbm, lens_in, in_sem.at[4]),
        pltpu.make_async_copy(slot_hbm, slot_in, in_sem.at[5]),
    ]
    for load in loads:
        load.start()

    row_i, col_i = iota((tok, tok), 0), iota((tok, tok), 1)
    swapped = (row_i // peer % nx) * blk + (row_i // blk) * peer + row_i % peer
    regroup = (swapped == col_i).astype(BF16)
    eye = (row_i == col_i).astype(F32)
    eye_low = eye.astype(BF16)

    loads[0].wait()
    s_g0[...] = mm(regroup, in_g[...]).astype(BF16)
    for load in loads[1:]:
        load.wait()
    pl.semaphore_wait(barrier, ny + nx - 1 + from_z)
    for zz in range(nz - 1):

        @pl.when((zz < z) & jnp.logical_not(late_line & (zz == 0)))
        def _():
            pl.semaphore_signal(ready, inc=1, device_id=at(y, x, zz), device_id_type=MESH)


    along("y", in_kv, y_kv, a_send.at[0], a_recv.at[0])
    along("y", in_q, y_q, a_send.at[1], a_recv.at[1])
    along("x", s_g0, x_g, a_send.at[2], a_recv.at[2])

    slot = slot_in[...]
    arrived = (slot // peer % nx) * blk + (slot // blk) * peer + slot % peer
    pos_col = jnp.sum(jnp.where(row_i == arrived, col_i.astype(F32), 0.0), axis=1, keepdims=True)
    pos_row = jnp.sum(eye * pos_col, axis=0, keepdims=True)
    lens_pad[...] = jnp.zeros_like(lens_pad)
    lens_pad[:, pl.ds(0, lens_in.shape[1])] = lens_in[...].astype(F32)
    lens = lens_pad[...]
    pad = lens.shape[1]
    below = iota((pad, pad), 1) <= iota((pad, pad), 0)
    ends_col = jnp.sum(jnp.where(below, lens, 0.0), axis=1, keepdims=True)
    first = (ctx * tok).astype(F32)
    doc_row = jnp.sum((ends_col <= pos_row + first).astype(F32), axis=0, keepdims=True)
    doc_col = jnp.sum(eye * doc_row, axis=1, keepdims=True)
    seen = (doc_col == doc_row) & (pos_col <= pos_row)
    own = jnp.where(seen, 0.0, NEG)
    later = jnp.where(lens[:, :1] >= first + tok, 0.0, NEG) + jnp.zeros((tok, tok), F32)
    bias[0, pl.ds(0, tok), :] = jnp.where(core == 0, own, later)
    bias[0, pl.ds(tok, tok), :] = jnp.where(core == 0, NEG, own)
    bias[1, pl.ds(0, tok), :] = later
    bias[1, pl.ds(tok, tok), :] = later
    m_row[...] = jnp.full_like(m_row, NEG)
    l_row[...] = jnp.zeros_like(l_row)
    o_t[...] = jnp.zeros_like(o_t)
    dq_t[...] = jnp.zeros_like(dq_t)

    drain(others(y_kv), a_recv.at[0])
    s_kv[...] = mm(regroup, y_kv[...]).astype(BF16)
    along("x", s_kv, kv_all.at[ctx], b_send.at[0], b_recv.at[0])
    drain(others(x_g), a_recv.at[2])
    s_g[...] = mm(regroup, x_g[...]).astype(BF16)
    along("y", s_g, g_all, b_send.at[2], b_recv.at[2])
    drain(others(y_q), a_recv.at[1])
    s_q[...] = mm(regroup, y_q[...]).astype(BF16)
    along("x", s_q, q_all, b_send.at[1], b_recv.at[1])

    def offset(t):
        return jnp.where(t % 2 == 1, (t + 1) // 2, (nz - t // 2) % nz)

    drain(others(s_kv), b_recv.at[0])

    def to_core(zz):
        here = kv_all.at[zz * 2 + core]
        remote(here, here, fwd_send.at[zz], fwd_recv.at[zz], sibling).start()

    @pl.when(jnp.logical_not(late) & (z < nz - 1))
    def _():
        pl.semaphore_wait(ready, nz - 1 - z)

    def kv_out(i, carry):
        o = i + 1

        @pl.when(z + o < nz)
        def _():
            remote(kv_all.at[ctx], kv_all.at[ctx], z_send.at[z + o], z_recv.at[z], at(y, x, z + o)).start()

        return carry

    lax.fori_loop(0, nz - 1, kv_out, 0)
    to_core(z)

    drain(others(q_all), b_recv.at[1])
    for h in range(heads):
        qf[pl.ds(h * tok, tok), :] = q_all[:, pl.ds(h * dh, dh)]
    drain(others(g_all), b_recv.at[2])
    for h in range(heads):
        grad = mm(regroup, g_all[:, pl.ds(h * dh, dh)]).astype(BF16)
        gf[pl.ds(h * tok, tok), :] = grad
        gt[:, pl.ds(h * tok, tok)] = mm_nt(eye_low, grad)

    def pair(zz):
        both = kv_all[pl.ds(zz * 2, 2)].reshape(2 * tok, 2 * dh)
        return both[:, :dh], both[:, dh:]

    def hop(t):
        return jnp.where((t == 0) | (t >= z), t, z - t)

    second = jnp.where(z <= 1, 1, z - 1)

    @pl.when(z >= second)
    def _():
        drain(s_kv, z_recv.at[z - second])
        to_core(z - second)

    def forward(t, carry):
        o = hop(t)
        nxt = hop(t + 2)

        @pl.when((t + 2 < nz) & (z >= nxt))
        def _():
            drain(s_kv, z_recv.at[z - nxt])
            to_core(z - nxt)

        @pl.when(z >= o)
        def _():
            zz = z - o
            drain(s_kv, fwd_recv.at[zz])
            key, value = pair(zz)
            shift = bias[jnp.minimum(o, 1)]
            score = mm_nt(key, qf[...]) * scale + jnp.concatenate([shift] * heads, axis=1)
            s_all[zz] = score
            dp_all[zz] = mm_nt(value, gf[...])
            old = m_row[...]
            new = jnp.maximum(old, jnp.max(score, axis=0, keepdims=True))
            weight = jnp.exp(score - new)
            fade = jnp.exp(old - new)
            m_row[...] = new
            l_row[...] = l_row[...] * fade + jnp.sum(weight, axis=0, keepdims=True)
            value_t = mm_nt(eye_low, value).astype(BF16)
            o_t[...] = o_t[...] * fade + mm(value_t, weight.astype(BF16))

        return carry

    lax.fori_loop(0, nz, forward, 0)

    attended_t = (o_t[...] * (1.0 / l_row[...])).astype(BF16)
    delta = jnp.sum(gt[...] * attended_t.astype(F32), axis=0, keepdims=True)
    log_total = m_row[...] + jnp.log(l_row[...])

    def send_x(i, value_t):
        for h in range(heads):
            x_out[i, :, pl.ds(h * dh, dh)] = mm_nt(eye_low, value_t[:, h * tok : (h + 1) * tok]).astype(BF16)
        along("x", x_out.at[i], r_out.at[i], xo_send.at[i], xo_recv.at[i])

    def send_y(i, dst):
        drain(others(r_out.at[i]), xo_recv.at[i])
        z_out[i] = mm(regroup, r_out[i]).astype(BF16)
        along("y", z_out.at[i], dst, yo_send.at[i], yo_recv.at[i])

    send_x(0, attended_t)

    def share(zz):
        drain(s_kv, part_recv.at[zz])
        comb[zz] = (part[zz, core].astype(F32) + sib_part[zz].astype(F32)).astype(BF16)
        remote(comb.at[zz], acc.at[z], acc_send.at[zz], acc_recv.at[z], at(y, x, zz)).start()

    def backward(i, carry):
        t = nz - 1 - i
        o = offset(t)
        last = offset(t + 3)

        @pl.when(z >= o)
        def _():
            zz = z - o
            key, value = pair(zz)
            prob = jnp.exp(s_all[zz] - log_total)
            score_grad = (prob * (dp_all[zz] - delta)).astype(BF16)
            key_t = mm_nt(eye_low, key).astype(BF16)
            value_part = mm(prob.astype(BF16), gf[...])
            key_part = mm(score_grad, qf[...]) * scale
            for b in range(2):
                part[zz, b, :, pl.ds(0, dh)] = key_part[b * tok : (b + 1) * tok].astype(BF16)
                part[zz, b, :, pl.ds(dh, dh)] = value_part[b * tok : (b + 1) * tok].astype(BF16)
            remote(part.at[zz, 1 - core], sib_part.at[zz], part_send.at[zz], part_recv.at[zz], sibling).start()
            dq_t[...] += mm(key_t, score_grad)

        @pl.when((t + 3 < nz) & (z >= last))
        def _():
            share(z - last)

        return carry

    lax.fori_loop(0, nz, backward, 0)

    if nz > 2:

        @pl.when(z >= nz - 1)
        def _():
            share(z - (nz - 1))

    @pl.when(z >= 1)
    def _():
        share(z - 1)

    send_x(1, (dq_t[...] * scale).astype(BF16))
    send_y(0, f_o)

    drain(s_kv, part_recv.at[z])
    total = part[z, core].astype(F32) + sib_part[z].astype(F32)
    for zz in range(nz):

        @pl.when(zz > z)
        def _():
            drain(s_kv, acc_recv.at[zz])

        @pl.when(zz <= z)
        def _():
            acc[zz] = jnp.zeros((tok, 2 * dh), BF16)

        total = total + acc[zz].astype(F32)
    s_dkv[...] = total.astype(BF16)
    along("x", s_dkv, r_dkv, xo_send.at[2], xo_recv.at[2])
    send_y(1, f_dq)
    drain(others(r_dkv), xo_recv.at[2])
    z_dkv[...] = mm(regroup, r_dkv[...]).astype(BF16)
    along("y", z_dkv, f_kv, yo_send.at[2], yo_recv.at[2])

    for i, (first_ref, second_ref) in enumerate(((in_kv, s_kv), (in_q, s_q), (s_g0, s_g))):
        drain(others(first_ref), a_send.at[i])
        drain(others(second_ref), b_send.at[i])
    for zz in range(nz):

        @pl.when(zz > z)
        def _():
            drain(s_kv, z_send.at[zz])

        @pl.when(zz < z)
        def _():
            drain(s_kv, acc_send.at[zz])

        @pl.when(zz <= z)
        def _():
            drain(s_kv, fwd_send.at[zz])
            drain(s_kv, part_send.at[zz])

    for i in range(2):
        drain(others(x_out.at[i]), xo_send.at[i])
        drain(others(z_out.at[i]), yo_send.at[i])
    drain(others(s_dkv), xo_send.at[2])
    drain(others(z_dkv), yo_send.at[2])
    drain(others(f_o), yo_recv.at[0])
    drain(others(f_dq), yo_recv.at[1])
    drain(others(f_kv), yo_recv.at[2])


def write_out(o_in, dq_in, kv_in, o_hbm, dq_hbm, dk_hbm, dv_hbm, sem):
    dh = dk_hbm.shape[1]
    copies = [
        pltpu.make_async_copy(o_in, o_hbm, sem.at[0]),
        pltpu.make_async_copy(dq_in, dq_hbm, sem.at[1]),
        pltpu.make_async_copy(kv_in.at[:, pl.ds(0, dh)], dk_hbm, sem.at[2]),
        pltpu.make_async_copy(kv_in.at[:, pl.ds(dh, dh)], dv_hbm, sem.at[3]),
    ]
    for copy in copies:
        copy.start()
    for copy in copies:
        copy.wait()


def local(ny, nx, nz, queries, keys, values, out_grad, doc_lengths, source_slot):
    tok, dh = keys.shape
    wide = queries.shape[1]
    heads = wide // dh
    flat = heads * tok
    docs = doc_lengths.shape[1]
    pad = -(-docs // 128) * 128
    dma = pltpu.SemaphoreType.DMA
    hbm = pl.BlockSpec(memory_space=pltpu.MemorySpace.HBM)
    vmem = pl.BlockSpec(memory_space=pltpu.VMEM)
    low = lambda *shape: pltpu.VMEM(shape, BF16)
    full = lambda *shape: pltpu.VMEM(shape, F32)
    whole = lambda *shape: pltpu.VMEM(shape, jnp.int32)
    found = pl.pallas_call(
        functools.partial(kernel, ny, nx, nz, heads),
        out_shape=(OUT(tok, wide), OUT(tok, wide), OUT(tok, 2 * dh)),
        in_specs=[hbm] * 6,
        out_specs=[vmem] * 3,
        scratch_shapes=[
            low(tok, 2 * dh), low(tok, wide), low(tok, wide), whole(1, docs), whole(1, tok),
            low(tok, 2 * dh), low(tok, wide), low(tok, wide),
            low(tok, 2 * dh), low(tok, wide), low(tok, wide), low(tok, wide),
            low(2 * nz, tok, 2 * dh), low(tok, wide), low(tok, wide),
            low(flat, dh), low(flat, dh), full(dh, flat),
            full(nz, 2 * tok, flat), full(nz, 2 * tok, flat),
            full(2, 2 * tok, tok), full(1, pad),
            full(1, flat), full(1, flat), full(dh, flat), full(dh, flat),
            low(2, tok, wide), low(2, tok, wide), low(2, tok, wide),
            low(nz, 2, tok, 2 * dh), low(nz, tok, 2 * dh), low(nz, tok, 2 * dh),
            low(nz, tok, 2 * dh), low(tok, 2 * dh), low(tok, 2 * dh), low(tok, 2 * dh),
            dma((6,)), dma((3,)), dma((3,)), dma((3,)), dma((3,)), dma((nz,)), dma((nz,)), dma((nz,)), dma((nz,)),
            dma((3,)), dma((3,)), dma((3,)), dma((3,)), dma((nz,)), dma((nz,)), dma((nz,)), dma((nz,)),
            pltpu.SemaphoreType.REGULAR,
        ],
        compiler_params=pltpu.CompilerParams(collective_id=0, has_side_effects=True),
        name="packed_attention",
    )(queries, keys, values, out_grad, doc_lengths, source_slot.reshape(1, tok))
    shapes = [(tok, wide), (tok, wide), (tok, dh), (tok, dh)]
    return pl.pallas_call(
        write_out,
        out_shape=tuple(jax.ShapeDtypeStruct(shape, BF16) for shape in shapes),
        in_specs=[vmem] * 3,
        out_specs=[hbm] * 4,
        scratch_shapes=[dma((4,))],
        name="write_out",
    )(*[pltpu.with_memory_space_constraint(each, pltpu.VMEM) for each in found])


def solution(mesh):
    side = math.isqrt(mesh.shape["dp"])
    placed = (
        P(("dp", "ctx"), None),
        P(("dp", "ctx"), None),
        P(("dp", "ctx"), None),
        P(("dp", "ctx"), None),
        P("dp", None),
        P(("dp", "ctx")),
    )
    return jax.shard_map(
        functools.partial(local, side, side, mesh.shape["ctx"] // 2),
        mesh=mesh,
        in_specs=placed,
        out_specs=(
            P(("dp", "ctx"), None),
            P(("dp", "ctx"), None),
            P(("dp", "ctx"), None),
            P(("dp", "ctx"), None),
        ),
        check_vma=False,
    )
```

```python
import functools
import math

import jax
import jax.numpy as jnp
from jax import lax
from jax.experimental import pallas as pl
from jax.experimental.pallas import tpu as pltpu
from jax.sharding import PartitionSpec as P

MESH = pl.DeviceIdType.MESH
NEG = -1e30
F32 = jnp.float32
BF16 = jnp.bfloat16


def OUT(*shape):
    return pltpu.VMEM(shape, BF16)


def mm(left, right):
    return jnp.dot(left, right, preferred_element_type=F32)


def mm_nt(left, right):
    return lax.dot_general(left, right, (((1,), (1,)), ((), ())), preferred_element_type=F32)


def iota(shape, dim):
    return lax.broadcasted_iota(jnp.int32, shape, dim)


def far_first(n):
    order = sorted(range(1, n), key=lambda k: -min(k, n - k))
    return order


def kernel(
    ny, nx, nz, heads,
    q_hbm, k_hbm, v_hbm, g_hbm, lens_hbm, slot_hbm,
    f_o, f_dq, f_kv,
    in_kv, in_q, in_g, lens_in, slot_in, y_kv, y_q, x_g, s_kv, s_q, s_g0, s_g, kv_all, q_all, g_all,
    qf, gf, gt, s_all, dp_all, bias, lens_pad, m_row, l_row, o_t, dq_t,
    x_out, r_out, z_out, part, sib_part, comb, acc, s_dkv, r_dkv, z_dkv,
    in_sem, a_send, a_recv, b_send, b_recv, z_send, z_recv, fwd_send, fwd_recv,
    xo_send, xo_recv, yo_send, yo_recv, part_send, part_recv, acc_send, acc_recv,
    ready,
):
    tok = in_kv.shape[0]
    dh = k_hbm.shape[1]
    wide = heads * dh
    peer = tok // (ny * nx)
    blk = tok // ny
    scale = dh ** -0.5
    dp = lax.axis_index("dp")
    ctx = lax.axis_index("ctx")
    y, x = dp // nx, dp % nx
    z, core = ctx // 2, ctx % 2
    sibling = (dp, z * 2 + 1 - core)

    def at(yy, xx, zz):
        return (yy * nx + xx, zz * 2 + core)

    def rows(i):
        return pl.ds(pl.multiple_of(i * blk, blk), blk)

    def remote(src, dst, send, recv, dev):
        return pltpu.make_async_remote_copy(
            src_ref=src, dst_ref=dst, send_sem=send, recv_sem=recv, device_id=dev, device_id_type=MESH
        )

    def drain(ref, sem):
        pltpu.make_async_copy(ref, ref, sem).wait()

    def others(ref):
        return ref.at[pl.ds(0, tok - blk)]

    def along(axis, src, dst, send, recv):
        me = y if axis == "y" else x
        n = ny if axis == "y" else nx
        for k in far_first(n):
            t = (me + k) % n
            dev = at(t, x, z) if axis == "y" else at(y, t, z)
            remote(src.at[rows(t)], dst.at[rows(me)], send, recv, dev).start()
        dst[rows(me), :] = src[rows(me), :]

    barrier = pltpu.get_barrier_semaphore()
    for k in far_first(ny):
        pl.semaphore_signal(barrier, inc=1, device_id=at((y + k) % ny, x, z), device_id_type=MESH)
    for k in far_first(nx):
        pl.semaphore_signal(barrier, inc=1, device_id=at(y, (x + k) % nx, z), device_id_type=MESH)
    pl.semaphore_signal(barrier, inc=1, device_id=sibling, device_id_type=MESH)
    late_line = (dp == 0) & (core == 0)
    late = late_line & (z == 0)
    for zz in range(1, nz):

        @pl.when((zz > z) & jnp.logical_not(late))
        def _():
            pl.semaphore_signal(barrier, inc=1, device_id=at(y, x, zz), device_id_type=MESH)

    @pl.when(late_line & (z > 0))
    def _():
        pl.semaphore_signal(barrier, inc=1, device_id=at(y, x, 0), device_id_type=MESH)

    from_z = jnp.where(late, nz - 1, jnp.where(late_line, z - 1, z))

    loads = [
        pltpu.make_async_copy(g_hbm, in_g, in_sem.at[0]),
        pltpu.make_async_copy(k_hbm, in_kv.at[:, pl.ds(0, dh)], in_sem.at[1]),
        pltpu.make_async_copy(v_hbm, in_kv.at[:, pl.ds(dh, dh)], in_sem.at[2]),
        pltpu.make_async_copy(q_hbm, in_q, in_sem.at[3]),
        pltpu.make_async_copy(lens_hbm, lens_in, in_sem.at[4]),
        pltpu.make_async_copy(slot_hbm, slot_in, in_sem.at[5]),
    ]
    for load in loads:
        load.start()

    row_i, col_i = iota((tok, tok), 0), iota((tok, tok), 1)
    swapped = (row_i // peer % nx) * blk + (row_i // blk) * peer + row_i % peer
    regroup = (swapped == col_i).astype(BF16)
    eye = (row_i == col_i).astype(F32)
    eye_low = eye.astype(BF16)

    for load in loads[1:]:
        load.wait()
    pl.semaphore_wait(barrier, ny + nx - 1 + from_z)
    for zz in range(nz - 1):

        @pl.when((zz < z) & jnp.logical_not(late_line & (zz == 0)))
        def _():
            pl.semaphore_signal(ready.at[z], inc=1, device_id=at(y, x, zz), device_id_type=MESH)


    along("y", in_kv, y_kv, a_send.at[0], a_recv.at[0])
    along("y", in_q, y_q, a_send.at[1], a_recv.at[1])
    loads[0].wait()
    s_g0[...] = mm(regroup, in_g[...]).astype(BF16)
    along("x", s_g0, x_g, a_send.at[2], a_recv.at[2])

    slot = slot_in[...]
    arrived = (slot // peer % nx) * blk + (slot // blk) * peer + slot % peer
    pos_col = jnp.sum(jnp.where(row_i == arrived, col_i.astype(F32), 0.0), axis=1, keepdims=True)
    pos_row = jnp.sum(eye * pos_col, axis=0, keepdims=True)
    lens_pad[...] = jnp.zeros_like(lens_pad)
    lens_pad[:, pl.ds(0, lens_in.shape[1])] = lens_in[...].astype(F32)
    lens = lens_pad[...]
    pad = lens.shape[1]
    below = iota((pad, pad), 1) <= iota((pad, pad), 0)
    ends_col = jnp.sum(jnp.where(below, lens, 0.0), axis=1, keepdims=True)
    first = (ctx * tok).astype(F32)
    doc_row = jnp.sum((ends_col <= pos_row + first).astype(F32), axis=0, keepdims=True)
    doc_col = jnp.sum(eye * doc_row, axis=1, keepdims=True)
    seen = (doc_col == doc_row) & (pos_col <= pos_row)
    own = jnp.where(seen, 0.0, NEG)
    later = jnp.where(lens[:, :1] >= first + tok, 0.0, NEG) + jnp.zeros((tok, tok), F32)
    bias[0, pl.ds(0, tok), :] = jnp.where(core == 0, own, later)
    bias[0, pl.ds(tok, tok), :] = jnp.where(core == 0, NEG, own)
    bias[1, pl.ds(0, tok), :] = later
    bias[1, pl.ds(tok, tok), :] = later
    m_row[...] = jnp.full_like(m_row, NEG)
    l_row[...] = jnp.zeros_like(l_row)
    o_t[...] = jnp.zeros_like(o_t)
    dq_t[...] = jnp.zeros_like(dq_t)

    drain(others(y_kv), a_recv.at[0])
    s_kv[...] = mm(regroup, y_kv[...]).astype(BF16)
    along("x", s_kv, kv_all.at[ctx], b_send.at[0], b_recv.at[0])
    drain(others(x_g), a_recv.at[2])
    s_g[...] = mm(regroup, x_g[...]).astype(BF16)
    along("y", s_g, g_all, b_send.at[2], b_recv.at[2])
    drain(others(y_q), a_recv.at[1])
    s_q[...] = mm(regroup, y_q[...]).astype(BF16)
    along("x", s_q, q_all, b_send.at[1], b_recv.at[1])

    def offset(t):
        return jnp.where(t % 2 == 1, (t + 1) // 2, (nz - t // 2) % nz)

    drain(others(s_kv), b_recv.at[0])

    def to_core(zz):
        here = kv_all.at[zz * 2 + core]
        remote(here, here, fwd_send.at[zz], fwd_recv.at[zz], sibling).start()

    def kv_out(i, carry):
        o = i + 1

        @pl.when((z + o < nz) & jnp.logical_not(late))
        def _():
            pl.semaphore_wait(ready.at[z + o], 1)

        @pl.when(z + o < nz)
        def _():
            remote(kv_all.at[ctx], kv_all.at[ctx], z_send.at[z + o], z_recv.at[z], at(y, x, z + o)).start()

        return carry

    lax.fori_loop(0, nz - 1, kv_out, 0)
    to_core(z)

    drain(others(q_all), b_recv.at[1])
    for h in range(heads):
        qf[pl.ds(h * tok, tok), :] = q_all[:, pl.ds(h * dh, dh)]
    drain(others(g_all), b_recv.at[2])
    for h in range(heads):
        grad = mm(regroup, g_all[:, pl.ds(h * dh, dh)]).astype(BF16)
        gf[pl.ds(h * tok, tok), :] = grad
        gt[:, pl.ds(h * tok, tok)] = mm_nt(eye_low, grad)

    def pair(zz):
        both = kv_all[pl.ds(zz * 2, 2)].reshape(2 * tok, 2 * dh)
        return both[:, :dh], both[:, dh:]

    def hop(t):
        return jnp.where((t == 0) | (t >= z), t, z - t)

    second = jnp.where(z <= 1, 1, z - 1)

    @pl.when(z >= second)
    def _():
        drain(s_kv, z_recv.at[z - second])
        to_core(z - second)

    def forward(t, carry):
        o = hop(t)
        nxt = hop(t + 2)

        @pl.when((t + 2 < nz) & (z >= nxt))
        def _():
            drain(s_kv, z_recv.at[z - nxt])
            to_core(z - nxt)

        @pl.when(z >= o)
        def _():
            zz = z - o
            drain(s_kv, fwd_recv.at[zz])
            key, value = pair(zz)
            shift = bias[jnp.minimum(o, 1)]
            score = mm_nt(key, qf[...]) * scale + jnp.concatenate([shift] * heads, axis=1)
            s_all[zz] = score
            dp_all[zz] = mm_nt(value, gf[...])
            old = m_row[...]
            new = jnp.maximum(old, jnp.max(score, axis=0, keepdims=True))
            weight = jnp.exp(score - new)
            fade = jnp.exp(old - new)
            m_row[...] = new
            l_row[...] = l_row[...] * fade + jnp.sum(weight, axis=0, keepdims=True)
            value_t = mm_nt(eye_low, value).astype(BF16)
            o_t[...] = o_t[...] * fade + mm(value_t, weight.astype(BF16))

        return carry

    lax.fori_loop(0, nz, forward, 0)

    attended_t = (o_t[...] * (1.0 / l_row[...])).astype(BF16)
    delta = jnp.sum(gt[...] * attended_t.astype(F32), axis=0, keepdims=True)
    log_total = m_row[...] + jnp.log(l_row[...])

    def send_x(i, value_t):
        for h in range(heads):
            x_out[i, :, pl.ds(h * dh, dh)] = mm_nt(eye_low, value_t[:, h * tok : (h + 1) * tok]).astype(BF16)
        along("x", x_out.at[i], r_out.at[i], xo_send.at[i], xo_recv.at[i])

    def send_y(i, dst):
        drain(others(r_out.at[i]), xo_recv.at[i])
        z_out[i] = mm(regroup, r_out[i]).astype(BF16)
        along("y", z_out.at[i], dst, yo_send.at[i], yo_recv.at[i])

    send_x(0, attended_t)

    def share(zz):
        drain(s_kv, part_recv.at[zz])
        comb[zz] = (part[zz, core].astype(F32) + sib_part[zz].astype(F32)).astype(BF16)
        remote(comb.at[zz], acc.at[z], acc_send.at[zz], acc_recv.at[z], at(y, x, zz)).start()

    def backward(i, carry):
        t = nz - 1 - i
        o = offset(t)
        last = offset(t + 3)

        @pl.when(z >= o)
        def _():
            zz = z - o
            key, value = pair(zz)
            prob = jnp.exp(s_all[zz] - log_total)
            score_grad = (prob * (dp_all[zz] - delta)).astype(BF16)
            key_t = mm_nt(eye_low, key).astype(BF16)
            value_part = mm(prob.astype(BF16), gf[...])
            key_part = mm(score_grad, qf[...]) * scale
            for b in range(2):
                part[zz, b, :, pl.ds(0, dh)] = key_part[b * tok : (b + 1) * tok].astype(BF16)
                part[zz, b, :, pl.ds(dh, dh)] = value_part[b * tok : (b + 1) * tok].astype(BF16)
            remote(part.at[zz, 1 - core], sib_part.at[zz], part_send.at[zz], part_recv.at[zz], sibling).start()
            dq_t[...] += mm(key_t, score_grad)

        @pl.when((t + 3 < nz) & (z >= last))
        def _():
            share(z - last)

        return carry

    lax.fori_loop(0, nz, backward, 0)

    if nz > 2:

        @pl.when(z >= nz - 1)
        def _():
            share(z - (nz - 1))

    @pl.when(z >= 1)
    def _():
        share(z - 1)

    send_x(1, (dq_t[...] * scale).astype(BF16))
    send_y(0, f_o)

    drain(s_kv, part_recv.at[z])
    total = part[z, core].astype(F32) + sib_part[z].astype(F32)
    for zz in range(nz):

        @pl.when(zz > z)
        def _():
            drain(s_kv, acc_recv.at[zz])

        @pl.when(zz <= z)
        def _():
            acc[zz] = jnp.zeros((tok, 2 * dh), BF16)

        total = total + acc[zz].astype(F32)
    s_dkv[...] = total.astype(BF16)
    along("x", s_dkv, r_dkv, xo_send.at[2], xo_recv.at[2])
    send_y(1, f_dq)
    drain(others(r_dkv), xo_recv.at[2])
    z_dkv[...] = mm(regroup, r_dkv[...]).astype(BF16)
    along("y", z_dkv, f_kv, yo_send.at[2], yo_recv.at[2])

    for i, (first_ref, second_ref) in enumerate(((in_kv, s_kv), (in_q, s_q), (s_g0, s_g))):
        drain(others(first_ref), a_send.at[i])
        drain(others(second_ref), b_send.at[i])
    for zz in range(nz):

        @pl.when(zz > z)
        def _():
            drain(s_kv, z_send.at[zz])

        @pl.when(zz < z)
        def _():
            drain(s_kv, acc_send.at[zz])

        @pl.when(zz <= z)
        def _():
            drain(s_kv, fwd_send.at[zz])
            drain(s_kv, part_send.at[zz])

    for i in range(2):
        drain(others(x_out.at[i]), xo_send.at[i])
        drain(others(z_out.at[i]), yo_send.at[i])
    drain(others(s_dkv), xo_send.at[2])
    drain(others(z_dkv), yo_send.at[2])
    drain(others(f_o), yo_recv.at[0])
    drain(others(f_dq), yo_recv.at[1])
    drain(others(f_kv), yo_recv.at[2])


def write_out(o_in, dq_in, kv_in, o_hbm, dq_hbm, dk_hbm, dv_hbm, sem):
    dh = dk_hbm.shape[1]
    copies = [
        pltpu.make_async_copy(o_in, o_hbm, sem.at[0]),
        pltpu.make_async_copy(dq_in, dq_hbm, sem.at[1]),
        pltpu.make_async_copy(kv_in.at[:, pl.ds(0, dh)], dk_hbm, sem.at[2]),
        pltpu.make_async_copy(kv_in.at[:, pl.ds(dh, dh)], dv_hbm, sem.at[3]),
    ]
    for copy in copies:
        copy.start()
    for copy in copies:
        copy.wait()


def local(ny, nx, nz, queries, keys, values, out_grad, doc_lengths, source_slot):
    tok, dh = keys.shape
    wide = queries.shape[1]
    heads = wide // dh
    flat = heads * tok
    docs = doc_lengths.shape[1]
    pad = -(-docs // 128) * 128
    dma = pltpu.SemaphoreType.DMA
    hbm = pl.BlockSpec(memory_space=pltpu.MemorySpace.HBM)
    vmem = pl.BlockSpec(memory_space=pltpu.VMEM)
    low = lambda *shape: pltpu.VMEM(shape, BF16)
    full = lambda *shape: pltpu.VMEM(shape, F32)
    whole = lambda *shape: pltpu.VMEM(shape, jnp.int32)
    found = pl.pallas_call(
        functools.partial(kernel, ny, nx, nz, heads),
        out_shape=(OUT(tok, wide), OUT(tok, wide), OUT(tok, 2 * dh)),
        in_specs=[hbm] * 6,
        out_specs=[vmem] * 3,
        scratch_shapes=[
            low(tok, 2 * dh), low(tok, wide), low(tok, wide), whole(1, docs), whole(1, tok),
            low(tok, 2 * dh), low(tok, wide), low(tok, wide),
            low(tok, 2 * dh), low(tok, wide), low(tok, wide), low(tok, wide),
            low(2 * nz, tok, 2 * dh), low(tok, wide), low(tok, wide),
            low(flat, dh), low(flat, dh), full(dh, flat),
            full(nz, 2 * tok, flat), full(nz, 2 * tok, flat),
            full(2, 2 * tok, tok), full(1, pad),
            full(1, flat), full(1, flat), full(dh, flat), full(dh, flat),
            low(2, tok, wide), low(2, tok, wide), low(2, tok, wide),
            low(nz, 2, tok, 2 * dh), low(nz, tok, 2 * dh), low(nz, tok, 2 * dh),
            low(nz, tok, 2 * dh), low(tok, 2 * dh), low(tok, 2 * dh), low(tok, 2 * dh),
            dma((6,)), dma((3,)), dma((3,)), dma((3,)), dma((3,)), dma((nz,)), dma((nz,)), dma((nz,)), dma((nz,)),
            dma((3,)), dma((3,)), dma((3,)), dma((3,)), dma((nz,)), dma((nz,)), dma((nz,)), dma((nz,)),
            pltpu.SemaphoreType.REGULAR((nz,)),
        ],
        compiler_params=pltpu.CompilerParams(collective_id=0, has_side_effects=True),
        name="packed_attention",
    )(queries, keys, values, out_grad, doc_lengths, source_slot.reshape(1, tok))
    shapes = [(tok, wide), (tok, wide), (tok, dh), (tok, dh)]
    return pl.pallas_call(
        write_out,
        out_shape=tuple(jax.ShapeDtypeStruct(shape, BF16) for shape in shapes),
        in_specs=[vmem] * 3,
        out_specs=[hbm] * 4,
        scratch_shapes=[dma((4,))],
        name="write_out",
    )(*[pltpu.with_memory_space_constraint(each, pltpu.VMEM) for each in found])


def solution(mesh):
    side = math.isqrt(mesh.shape["dp"])
    placed = (
        P(("dp", "ctx"), None),
        P(("dp", "ctx"), None),
        P(("dp", "ctx"), None),
        P(("dp", "ctx"), None),
        P("dp", None),
        P(("dp", "ctx")),
    )
    return jax.shard_map(
        functools.partial(local, side, side, mesh.shape["ctx"] // 2),
        mesh=mesh,
        in_specs=placed,
        out_specs=(
            P(("dp", "ctx"), None),
            P(("dp", "ctx"), None),
            P(("dp", "ctx"), None),
            P(("dp", "ctx"), None),
        ),
        check_vma=False,
    )
```
